32 devices in a mesh: gx: 4 (over y, x), gy: 8 (over z, core).
Axes of the slice: x: 2, y: 2, z: 4, core: 2. Of those that a mesh axis runs over, the one named last changes fastest.
Arguments:
- start_block: bfloat16 [64, 65536], P(None, ('gx', 'gy')), may hold values from -200 to 200
- tiles: bfloat16 [256, 10, 256, 256], P(('gx', 'gy')), may hold values from -0.125 to 0.125
- tile_cols: int32 [256, 10], P(('gx', 'gy')), may hold values from 0 to 15, as said below
- send_rows: int32 [32, 2], P(('gx', 'gy')), may hold values from 0 to 7, as said below
- shifts: float32 [4], replicated, may hold values from -1 to 1
Outputs:
- basis_q: float32 [256, 65536], P(None, ('gx', 'gy'))
The draws below stay inside these ranges and needn't reach their ends.
Inputs may be any that keep to these rules, and one draw needn't show every extreme that they name: `tile_cols`: every tile-row's first tile is its own diagonal tile; values below 8 name the partition's own tile-rows, the others ghost slots in the extended order. `send_rows`: each partition's 2 entries are distinct own tile-rows.
All inputs are finite; a program needn't handle non-finite values.
Results may differ from the reference program's by a relative error of at most 0.009.
The reference program's roundings to bfloat16 on the way count: a program that leaves them out, or rounds other values in their place, can miss the bound.
Values may be sent and summed in bfloat16 or wider, within the bound.
A program may use at most 64 MiB of HBM per device.

```python
import jax
import jax.numpy as jnp
from jax import lax

TILE = 256
BLOCK = 64
STEPS = 4
TR_DEV = 8
K = 10
GHOSTS = 2
NT = 256
NROWS = 65536
N_GX = 4
N_GY = 8
DEVICES = 32


def draw_start_block(key, part):
    noise_key = jax.random.fold_in(key, 0)
    values = jnp.clip(jax.random.normal(noise_key, (BLOCK, NROWS), jnp.float32), -6.0, 6.0)
    return values.astype(jnp.bfloat16)


def draw_tile_cols(key, part):
    local = jnp.arange(NT, dtype=jnp.int32) % TR_DEV
    first = local[:, None]
    second = (TR_DEV + local % (4 * GHOSTS))[:, None]
    rest = jax.random.randint(key, (NT, K - 2), 0, TR_DEV + 4 * GHOSTS, dtype=jnp.int32)
    return jnp.concatenate([first, second, rest], axis=1).astype(jnp.int32)


def draw_send_rows(key, part):
    keys = jax.random.split(key, DEVICES)
    perms = jax.vmap(lambda k: jax.random.permutation(k, TR_DEV))(keys).astype(jnp.int32)
    chosen = perms[:, :GHOSTS]
    fixed_row = jnp.roll(jnp.arange(TR_DEV, dtype=jnp.int32), 1)[:GHOSTS]
    return chosen.at[0].set(fixed_row).astype(jnp.int32)


def level_of(stream_key, extent, cuts, least, top_value):
    factor_of, own = 1.0, jax.random.fold_in(stream_key, 6)
    for axis_at, blocks in cuts:
        heights = jnp.exp(jax.random.uniform(jax.random.fold_in(own, axis_at), (blocks,), jnp.float32, least / len(cuts), top_value / len(cuts)))
        factor_of = factor_of * jnp.repeat(heights, extent[axis_at] // blocks).reshape([-1 if axis == axis_at else 1 for axis in range(len(extent))])
    return factor_of


def scatter_about(rng, extent, deviation, limit, pieces=(), kind=jnp.bfloat16):
    array = deviation * jax.random.normal(rng, extent, jnp.float32)
    if pieces:
        array = array * level_of(rng, extent, pieces, -0.22, 0.18)
    return jnp.clip(array, -limit, limit).astype(kind)


def setup_inputs(seed: int = 0) -> dict:
    key_list = jax.random.split(jax.random.key(seed), 6)
    start_block = draw_start_block(jax.random.fold_in(key_list[5], 71), 0)
    tiles = scatter_about(key_list[1], (NT, K, TILE, TILE), (TILE * K) ** -0.5, 0.125, ((0, 32),))
    tile_cols = draw_tile_cols(jax.random.fold_in(key_list[5], 71), 0)
    send_rows = draw_send_rows(jax.random.fold_in(key_list[5], 71), 0)
    shifts = jnp.clip(jax.random.uniform(key_list[4], (STEPS,), jnp.float32, -1.0, 1.0), -1.0, 1.0)
    return dict(start_block=start_block, tiles=tiles, tile_cols=tile_cols, send_rows=send_rows, shifts=shifts)


def apply_operator(current, tiles, tile_cols, send_rows):
    parts = N_GX * N_GY
    own = current.reshape(BLOCK, parts, TR_DEV, TILE)
    flat = (jnp.arange(parts, dtype=jnp.int32)[:, None] * TR_DEV + send_rows).reshape(-1).astype(jnp.int32)
    outgoing = jnp.take(own.reshape(BLOCK, parts * TR_DEV, TILE), flat, axis=1)
    outgoing = outgoing.reshape(BLOCK, N_GX, N_GY, GHOSTS, TILE)
    padded = jnp.pad(outgoing, ((0, 0), (1, 1), (1, 1), (0, 0), (0, 0)))
    from_xm = padded[:, :-2, 1:-1]
    from_xp = padded[:, 2:, 1:-1]
    from_ym = padded[:, 1:-1, :-2]
    from_yp = padded[:, 1:-1, 2:]
    own_grid = own.reshape(BLOCK, N_GX, N_GY, TR_DEV, TILE)
    extended = jnp.concatenate([own_grid, from_xm, from_xp, from_ym, from_yp], axis=3)
    extended = extended.reshape(BLOCK, parts, TR_DEV + 4 * GHOSTS, TILE)
    cols = tile_cols.reshape(parts, TR_DEV * K)
    tile_parts = tiles.reshape(parts, TR_DEV, K, TILE, TILE)

    def apply_part(index):
        ext = lax.dynamic_index_in_dim(extended, index, 1, keepdims=False)
        picked = jnp.take(ext, cols[index], axis=1).reshape(BLOCK, TR_DEV, K, TILE)
        return jnp.einsum('ctkb,tkab->cta', picked.astype(jnp.float32), tile_parts[index].astype(jnp.float32), precision=lax.Precision.HIGHEST)
    image = lax.map(apply_part, jnp.arange(parts, dtype=jnp.int32))
    return jnp.transpose(image, (1, 0, 2, 3)).reshape(BLOCK, NROWS)

def reference(start_block, tiles, tile_cols, send_rows, shifts):
    current = start_block
    blocks = []
    for step in range(STEPS):
        image = apply_operator(current, tiles, tile_cols, send_rows)
        current = (image - shifts[step] * current.astype(jnp.float32)).astype(jnp.bfloat16)
        blocks.append(current)
    basis = jnp.concatenate(blocks, axis=0)
    gram = lax.dot_general(basis.astype(jnp.float32), basis.astype(jnp.float32), (((1,), (1,)), ((), ())), preferred_element_type=jnp.float32) / NROWS
    lower = jnp.linalg.cholesky(gram)
    return lax.linalg.triangular_solve(lower, basis.astype(jnp.float32), left_side=True, lower=True)
```

```python
import functools

import jax
import jax.numpy as jnp
from jax import lax
from jax.experimental import pallas as pl
from jax.experimental.pallas import tpu as pltpu
from jax.sharding import PartitionSpec as P

MESH = pl.DeviceIdType.MESH
F32 = jnp.float32
BF16 = jnp.bfloat16
NT_DIMS = (((1,), (1,)), ((), ()))
LANES = 128
PIECE = 4


def nt(a, b, precision=None):
    return lax.dot_general(a, b, NT_DIMS, precision=precision, preferred_element_type=F32)


def split_dot(left, right):
    rows = left.shape[0]
    main = left.astype(BF16)
    rest = (left - main.astype(F32)).astype(BF16)
    both = jnp.dot(jnp.concatenate([main, rest], axis=0), right, preferred_element_type=F32)
    return both[:rows] + both[rows:]


def relay_rounds(nx, ny):
    rounds = []
    d = 1
    while d < max(nx, ny):
        near = [(0, d), (0, -d)] if d < ny else []
        near += [(d, 0), (-d, 0)] if d < nx else []
        rounds.append(near)
        d *= 2
    rounds.append([(s * d, 0) for d in range(1, nx) for s in (1, -1)])
    return rounds


def krylov_kernel(dims, send_rows, tile_cols, shifts, start, tiles_hbm, basis_out, early_out, gram, above, *scratch):
    nx, ny, steps, tile_rows, slots, ghosts, tile, width, total = dims
    sums = steps - 1
    count = nx * ny
    span = gram.shape[1]
    per_column = width // PIECE
    parts = per_column * (span // LANES)
    stride = count // parts
    (tiles, basis, early, first, tile_sem, out_sem, early_sem, halo_send, halo_recv, relay,
     rs_send, rs_recv, ag_send, ag_recv) = scratch[:14]
    ext = scratch[14:14 + steps]
    outbox = scratch[14 + steps:14 + 2 * steps]
    part = scratch[14 + 2 * steps:14 + 2 * steps + sums]
    landed = scratch[14 + 2 * steps + sums:14 + 2 * steps + 2 * sums]
    full = scratch[14 + 2 * steps + 2 * sums:14 + 2 * steps + 3 * sums]
    ix, iy = lax.axis_index("gx"), lax.axis_index("gy")
    me = ix * ny + iy

    def place(r):
        return (r // ny, lax.rem(r, ny))

    def tile_copy(t):
        return pltpu.make_async_copy(tiles_hbm.at[t], tiles.at[t], tile_sem.at[t])

    for t in range(tile_rows):
        tile_copy(t).start()

    def inside(dx, dy):
        x, y = ix + dx, iy + dy
        return (x >= 0) & (x < nx) & (y >= 0) & (y < ny)

    def tell(sem, offsets):
        for dx, dy in offsets:
            @pl.when(inside(dx, dy))
            def _():
                pl.semaphore_signal(sem, inc=1, device_id=(ix + dx, iy + dy), device_id_type=MESH)

    def heard(sem, offsets):
        pl.semaphore_wait(sem, sum(jnp.where(inside(dx, dy), 1, 0) for dx, dy in offsets))

    sides = [(0, 1), (0, -1), (1, 0), (-1, 0)]
    slot_of = {(1, 0): 0, (-1, 0): 1, (0, 1): 2, (0, -1): 3}
    barrier = pltpu.get_barrier_semaphore()
    tell(barrier, sides)

    for t in range(tile_rows):
        rows = start[:, t * tile:(t + 1) * tile]
        ext[0][t] = rows
        first[t] = rows
    for s in range(ghosts):
        outbox[0][s] = first[send_rows[0, s]]

    def edges(j):
        for dx, dy in sides:
            low = tile_rows + slot_of[dx, dy] * ghosts

            @pl.when(jnp.logical_not(inside(-dx, -dy)))
            def _():
                ext[j][low:low + ghosts] = jnp.zeros((ghosts, width, tile), BF16)

    for j in range(steps):
        edges(j)
    heard(barrier, sides)

    def halo(j, s):
        out = []
        for n, (dx, dy) in enumerate(sides):
            low = tile_rows + slot_of[dx, dy] * ghosts
            copy = pltpu.make_async_remote_copy(
                src_ref=outbox[j].at[s], dst_ref=ext[j].at[low + s],
                send_sem=halo_send.at[j, s, n], recv_sem=halo_recv.at[j, s, n],
                device_id=(ix + dx, iy + dy), device_id_type=MESH)
            out.append((inside(dx, dy), inside(-dx, -dy), copy))
        return out

    def halo_start(j, s):
        for sends, _, copy in reversed(halo(j, s)):
            pl.when(sends)(copy.start)

    def halo_wait(j):
        for s in range(ghosts):
            for _, receives, copy in halo(j, s):
                pl.when(receives)(copy.wait_recv)

    def halo_drain(j):
        for s in range(ghosts):
            for sends, _, copy in halo(j, s):
                pl.when(sends)(copy.wait_send)

    for s in range(ghosts):
        halo_start(0, s)

    rounds = relay_rounds(nx, ny)
    tell(relay.at[0], rounds[0])
    pending = [0]

    def relay_turn():
        r = pending[0]
        if r < len(rounds):
            heard(relay.at[r], rounds[r])
            if r + 1 < len(rounds):
                tell(relay.at[r + 1], rounds[r + 1])
            pending[0] = r + 1

    def turned(t, c):
        tile_copy(t).wait()
        for k in range(slots):
            tiles[t, k] = tiles[t, k].T
        return c

    half = tile_rows // 2
    lax.fori_loop(0, half, turned, 0)
    relay_turn()
    lax.fori_loop(half, tile_rows, turned, 0)
    basis[(steps - 1) * width:, :] = jnp.zeros((width, basis.shape[1]), BF16)
    relay_turn()

    def row_image(j, r):
        acc = jnp.dot(ext[j][tile_cols[r, 0]], tiles[r, 0], preferred_element_type=F32)
        for k in range(1, slots):
            acc = acc + jnp.dot(ext[j][tile_cols[r, k]], tiles[r, k], preferred_element_type=F32)
        return (acc - shifts[j] * ext[j][r].astype(F32)).astype(BF16)

    def own_part():
        return me // stride

    def when_owner(act):
        if stride == 1:
            act()
        else:
            pl.when(lax.rem(me, stride) == 0)(act)

    def rs_copy(u, q):
        p = lax.rem(own_part() + q, parts)
        owner = p * stride
        return owner, pltpu.make_async_remote_copy(
            src_ref=part[u].at[p], dst_ref=landed[u].at[lax.rem(me - owner + count, count) - 1],
            send_sem=rs_send.at[u], recv_sem=rs_recv.at[u],
            device_id=place(owner), device_id_type=MESH)

    def ag_copy(u, d):
        p = own_part()
        return pltpu.make_async_remote_copy(
            src_ref=full[u].at[p], dst_ref=full[u].at[p],
            send_sem=ag_send.at[u], recv_sem=ag_recv.at[u],
            device_id=place(lax.rem(me + d, count)), device_id_type=MESH)

    def scatter(u):
        def send(q, c):
            owner, copy = rs_copy(u, q)
            if stride == 1:
                copy.start()
            else:
                pl.when(owner != me)(copy.start)
            return c
        lax.fori_loop(1 if stride == 1 else 0, parts, send, 0)

    def arrived(ref, sem):
        pltpu.make_async_copy(ref, ref, sem).wait()

    def gather(u):
        def act():
            arrived(landed[u], rs_recv.at[u])
            full[u][own_part()] = (jnp.sum(landed[u][...], axis=0) + part[u][own_part()]) / total

            def send(d, c):
                ag_copy(u, d).start()
                return c
            lax.fori_loop(1, count, send, 0)
        when_owner(act)

    def but_own(act_all, act_rest):
        if stride == 1:
            act_rest()
        else:
            own = lax.rem(me, stride) == 0
            pl.when(own)(act_rest)
            pl.when(jnp.logical_not(own))(act_all)

    def collect(u):
        but_own(lambda: arrived(full[u], ag_recv.at[u]),
                lambda: arrived(full[u].at[:parts - 1], ag_recv.at[u]))

    def drain(u):
        but_own(lambda: arrived(part[u], rs_send.at[u]),
                lambda: arrived(part[u].at[:parts - 1], rs_send.at[u]))
        when_owner(lambda: arrived(landed[u], ag_send.at[u]))

    def column(u, c):
        low = c * per_column
        return jnp.concatenate([full[u][p] for p in range(low, low + per_column)], axis=0)

    def load_part(u, blocks):
        for c, block in enumerate(blocks):
            for a in range(per_column):
                part[u][c * per_column + a] = block[a * PIECE:(a + 1) * PIECE]

    def basis_copy(j):
        rows = slice(j * width, (j + 1) * width)
        return pltpu.make_async_copy(basis.at[rows], basis_out.at[rows], out_sem.at[j])

    for j in range(steps):
        halo_wait(j)
        if j + 1 < steps:
            for s in range(ghosts):
                outbox[j + 1][s] = row_image(j, send_rows[0, s])
                halo_start(j + 1, s)

        def row(t, c):
            value = row_image(j, t)
            if j + 1 < steps:
                ext[j + 1][t] = value
            basis[j * width:(j + 1) * width, pl.ds(pl.multiple_of(t * tile, tile), tile)] = value
            return c

        lax.fori_loop(0, tile_rows, row, 0, unroll=8)
        basis_copy(j).start()
        if j == 0:
            relay_turn()
        elif j == 1:
            local = nt(basis[:2 * width, :], basis[:2 * width, :])
            load_part(0, [local[:width], local[width:]])
            for _ in rounds:
                relay_turn()
            scatter(0)
        else:
            local = nt(basis[j * width:(j + 1) * width, :], basis[...])
            load_part(j - 1, [local[:, c * LANES:(c + 1) * LANES] for c in range(span // LANES)])
            scatter(j - 1)
            gather(j - 2)
    above[...] = jnp.zeros(above.shape, F32)
    collect(0)
    extend_inverse(0, width, column(0, 0)[:, :width], above)
    extend_inverse(1, width, column(0, 1), above)
    gather(steps - 2)
    for u in range(1, steps - 2):
        collect(u)
        wide = jnp.concatenate([column(u, c) for c in range(span // LANES)], axis=1)
        extend_inverse(u + 1, width, wide[:, :(u + 2) * width], above)
    done = (steps - 1) * width
    chunk = 2 * tile
    for n in range(basis.shape[1] // chunk):
        cols = slice(n * chunk, (n + 1) * chunk)
        early[:, cols] = split_dot(above[:done, :], basis[:, cols])
    early_copy = pltpu.make_async_copy(early, early_out, early_sem)
    early_copy.start()
    collect(steps - 2)
    for c in range(span // LANES):
        gram[:, c * LANES:(c + 1) * LANES] = column(steps - 2, c)
    early_copy.wait()
    for j in range(steps):
        basis_copy(j).wait()
        halo_drain(j)
    for u in range(sums):
        drain(u)


def factor(block, midway=None):
    width = block.shape[0]
    count = width // 8
    eye_r = lax.broadcasted_iota(jnp.int32, (width, width), 0)
    eye_c = lax.broadcasted_iota(jnp.int32, (width, width), 1)
    work = jnp.concatenate([block, jnp.where(eye_r == eye_c, 1.0, 0.0).astype(F32)], axis=1)
    rows = lax.broadcasted_iota(jnp.int32, (8, 2 * width), 0)
    groups = [work[g * 8:(g + 1) * 8] for g in range(count)]
    done = []
    for g in range(count):
        if midway is not None and g == count // 2:
            midway()
        cols = [
            [jnp.broadcast_to(groups[h][:, g * 8 + r:g * 8 + r + 1], (8, 2 * width)) for h in range(g, count)]
            for r in range(8)
        ]
        pivots = cols[0][0]
        for r in range(8):
            inverse = 1.0 / cols[r][0][r:r + 1]
            if r:
                pivots = jnp.where(rows == r, cols[r][0], pivots)
            for m in range(r + 1, 8):
                share = cols[m][0][r:r + 1] * inverse
                cols[m] = [c - d * share for c, d in zip(cols[m], cols[r])]
            scaled = groups[g][r:r + 1] * inverse
            for h in range(g, count):
                update = groups[h] - cols[r][h - g] * scaled
                groups[h] = jnp.where(rows > r, update, groups[h]) if h == g else update
        done.append(groups[g] * lax.rsqrt(pivots))
    return jnp.concatenate(done, axis=0)[:, width:]


def extend_inverse(j, width, gram_row, inverse, midway=None):
    high = lax.Precision.HIGHEST
    lo, hi = j * width, (j + 1) * width
    block = gram_row[:, lo:hi]
    if j:
        previous = inverse[0:lo, 0:lo]
        left = nt(gram_row[:, 0:lo], previous, high)
        block = block - nt(left, left, high)
    own = factor(block, midway)
    inverse[lo:hi, lo:hi] = own
    if j:
        cross = jnp.dot(left, previous, precision=high, preferred_element_type=F32)
        inverse[lo:hi, 0:lo] = -jnp.dot(own, cross, precision=high, preferred_element_type=F32)


def finish_kernel(dims, basis_hbm, early_hbm, gram, above, out, inverse, basis, early, staged, sem):
    steps, width, chunk = dims
    done = (steps - 1) * width
    early_in = pltpu.make_async_copy(early_hbm, early, sem.at[0])
    early_in.start()
    basis_copy = pltpu.make_async_copy(basis_hbm, basis, sem.at[1])
    basis_copy.start()
    early_copy = pltpu.make_async_copy(early, out.at[:done], sem.at[2])

    def pass_on():
        early_in.wait()
        early_copy.start()

    inverse[:done] = above[...]
    extend_inverse(steps - 1, width, gram[...], inverse, pass_on)
    basis_copy.wait()
    copies = []
    for n in range(basis.shape[1] // chunk):
        cols = slice(n * chunk, (n + 1) * chunk)
        staged[:, cols] = split_dot(inverse[done:, :], basis[:, cols])
        copy = pltpu.make_async_copy(staged.at[:, cols], out.at[done:, cols], sem.at[3 + n])
        copy.start()
        copies.append(copy)
    early_copy.wait()
    for copy in copies:
        copy.wait()


def body(nx, ny, start_block, tiles, tile_cols, send_rows, shifts):
    width, nodes = start_block.shape
    tile_rows, slots, tile, _ = tiles.shape
    ghosts = send_rows.shape[1]
    steps = shifts.shape[0]
    size = steps * width
    done = size - width
    sums = steps - 1
    span = -(-size // LANES) * LANES
    parts = (width // PIECE) * (span // LANES)
    count = nx * ny
    dims = (nx, ny, steps, tile_rows, slots, ghosts, tile, width, nodes * count)
    dma = pltpu.SemaphoreType.DMA
    vmem = pl.BlockSpec(memory_space=pltpu.VMEM)
    smem = pl.BlockSpec(memory_space=pltpu.SMEM)
    hbm = pl.BlockSpec(memory_space=pl.ANY)
    basis, early, gram, above = pl.pallas_call(
        functools.partial(krylov_kernel, dims),
        out_shape=(
            jax.ShapeDtypeStruct((size, nodes), BF16),
            jax.ShapeDtypeStruct((done, nodes), F32),
            jax.ShapeDtypeStruct((width, span), F32),
            jax.ShapeDtypeStruct((done, size), F32),
        ),
        in_specs=[smem, smem, smem, vmem, hbm],
        out_specs=(hbm, hbm, vmem, vmem),
        scratch_shapes=[
            pltpu.VMEM(tiles.shape, BF16),
            pltpu.VMEM((size, nodes), BF16),
            pltpu.VMEM((done, nodes), F32),
            pltpu.VMEM((tile_rows, width, tile), BF16),
            dma((tile_rows,)), dma((steps,)), dma,
            dma((steps, ghosts, 4)), dma((steps, ghosts, 4)),
            pltpu.SemaphoreType.REGULAR((len(relay_rounds(nx, ny)),)),
            dma((sums,)), dma((sums,)), dma((sums,)), dma((sums,)),
        ]
        + [pltpu.VMEM((tile_rows + 4 * ghosts, width, tile), BF16) for _ in range(steps)]
        + [pltpu.VMEM((ghosts, width, tile), BF16) for _ in range(steps)]
        + [pltpu.VMEM((parts, PIECE, LANES), F32) for _ in range(sums)]
        + [pltpu.VMEM((count - 1, PIECE, LANES), F32) for _ in range(sums)]
        + [pltpu.VMEM((parts, PIECE, LANES), F32) for _ in range(sums)],
        compiler_params=pltpu.CompilerParams(collective_id=0, has_side_effects=True, vmem_limit_bytes=56 * 2**20),
    )(send_rows, tile_cols, shifts, start_block, tiles)
    chunk = 2 * tile
    return pl.pallas_call(
        functools.partial(finish_kernel, (steps, width, chunk)),
        out_shape=jax.ShapeDtypeStruct((size, nodes), F32),
        in_specs=[hbm, hbm, vmem, vmem],
        out_specs=hbm,
        scratch_shapes=[
            pltpu.VMEM((size, size), F32),
            pltpu.VMEM((size, nodes), BF16),
            pltpu.VMEM((done, nodes), F32),
            pltpu.VMEM((width, nodes), F32),
            dma((3 + nodes // chunk,)),
        ],
        compiler_params=pltpu.CompilerParams(vmem_limit_bytes=56 * 2**20),
    )(basis, early, gram, above)


def solution(mesh):
    in_specs = (
        P(None, ("gx", "gy")),
        P(("gx", "gy"), None, None, None),
        P(("gx", "gy"), None),
        P(("gx", "gy"), None),
        P(),
    )
    out_specs = P(None, ("gx", "gy"))
    run = functools.partial(body, mesh.shape["gx"], mesh.shape["gy"])
    return jax.shard_map(run, mesh=mesh, in_specs=in_specs, out_specs=out_specs, check_vma=False)
```

```python
import functools

import jax
import jax.numpy as jnp
from jax import lax
from jax.experimental import pallas as pl
from jax.experimental.pallas import tpu as pltpu
from jax.sharding import PartitionSpec as P

MESH = pl.DeviceIdType.MESH
F32 = jnp.float32
BF16 = jnp.bfloat16
NT_DIMS = (((1,), (1,)), ((), ()))
LANES = 128
PIECE = 4


def nt(a, b, precision=None):
    return lax.dot_general(a, b, NT_DIMS, precision=precision, preferred_element_type=F32)


def split_dot(left, right):
    rows = left.shape[0]
    main = left.astype(BF16)
    rest = (left - main.astype(F32)).astype(BF16)
    both = jnp.dot(jnp.concatenate([main, rest], axis=0), right, preferred_element_type=F32)
    return both[:rows] + both[rows:]


def relay_rounds(nx, ny):
    rounds = []
    d = 1
    while d < max(nx, ny):
        near = [(0, d), (0, -d)] if d < ny else []
        near += [(d, 0), (-d, 0)] if d < nx else []
        rounds.append(near)
        d *= 2
    rounds.append([(s * d, 0) for d in range(1, nx) for s in (1, -1)])
    return rounds


def krylov_kernel(dims, send_rows, tile_cols, shifts, start, tiles_hbm, basis_out, early_out, gram, above, *scratch):
    nx, ny, steps, tile_rows, slots, ghosts, tile, width, total = dims
    sums = steps - 1
    count = nx * ny
    span = gram.shape[1]
    per_column = width // PIECE
    parts = per_column * (span // LANES)
    stride = count // parts
    (tiles, basis, early, first, tile_sem, out_sem, early_sem, halo_send, halo_recv, relay,
     rs_send, rs_recv, ag_send, ag_recv) = scratch[:14]
    ext = scratch[14:14 + steps]
    outbox = scratch[14 + steps:14 + 2 * steps]
    part = scratch[14 + 2 * steps:14 + 2 * steps + sums]
    landed = scratch[14 + 2 * steps + sums:14 + 2 * steps + 2 * sums]
    full = scratch[14 + 2 * steps + 2 * sums:14 + 2 * steps + 3 * sums]
    ix, iy = lax.axis_index("gx"), lax.axis_index("gy")
    me = ix * ny + iy

    def place(r):
        return (r // ny, lax.rem(r, ny))

    def tile_copy(t):
        return pltpu.make_async_copy(tiles_hbm.at[t], tiles.at[t], tile_sem.at[t])

    for t in range(tile_rows):
        tile_copy(t).start()

    def inside(dx, dy):
        x, y = ix + dx, iy + dy
        return (x >= 0) & (x < nx) & (y >= 0) & (y < ny)

    def tell(sem, offsets):
        for dx, dy in offsets:
            @pl.when(inside(dx, dy))
            def _():
                pl.semaphore_signal(sem, inc=1, device_id=(ix + dx, iy + dy), device_id_type=MESH)

    def heard(sem, offsets):
        pl.semaphore_wait(sem, sum(jnp.where(inside(dx, dy), 1, 0) for dx, dy in offsets))

    sides = [(0, 1), (0, -1), (1, 0), (-1, 0)]
    slot_of = {(1, 0): 0, (-1, 0): 1, (0, 1): 2, (0, -1): 3}
    barrier = pltpu.get_barrier_semaphore()
    tell(barrier, sides)

    for t in range(tile_rows):
        rows = start[:, t * tile:(t + 1) * tile]
        ext[0][t] = rows
        first[t] = rows
    for s in range(ghosts):
        outbox[0][s] = first[send_rows[0, s]]

    def edges(j):
        for dx, dy in sides:
            low = tile_rows + slot_of[dx, dy] * ghosts

            @pl.when(jnp.logical_not(inside(-dx, -dy)))
            def _():
                ext[j][low:low + ghosts] = jnp.zeros((ghosts, width, tile), BF16)

    for j in range(steps):
        edges(j)
    heard(barrier, sides)

    far = jnp.where(lax.rem(ix, 2) == 1, 1, -1)
    far_pair = (far, 0, jnp.where(far == 1, 0, 1), jnp.where(far == 1, 1, 0), 0)
    near_pair = (-far, 0, jnp.where(far == 1, 1, 0), jnp.where(far == 1, 0, 1), 1)
    up_pair = (0, 1, 2, 2, 2)
    down_pair = (0, -1, 3, 3, 3)
    pairs = (far_pair, up_pair, down_pair, near_pair)

    def halo(j, s, pair, incoming=False):
        dx, dy, lands, comes, n = pair
        return pltpu.make_async_remote_copy(
            src_ref=outbox[j].at[s],
            dst_ref=ext[j].at[tile_rows + (comes if incoming else lands) * ghosts + s],
            send_sem=halo_send.at[j, s, n], recv_sem=halo_recv.at[j, s, n],
            device_id=(ix + dx, iy + dy), device_id_type=MESH)

    def halo_start(j, s, some):
        for pair in some:
            @pl.when(inside(pair[0], pair[1]))
            def _():
                halo(j, s, pair).start()

    def halo_wait(j):
        for pair in pairs:
            back = 1 if pair[1] == 0 else -1

            @pl.when(inside(pair[0], back * pair[1]))
            def _():
                for s in range(ghosts):
                    halo(j, s, pair, True).wait_recv()

    def halo_drain(j):
        for pair in pairs:
            @pl.when(inside(pair[0], pair[1]))
            def _():
                for s in range(ghosts):
                    halo(j, s, pair).wait_send()

    for s in range(ghosts):
        halo_start(0, s, pairs[:1])
    for s in range(ghosts):
        halo_start(0, s, pairs[1:])

    rounds = relay_rounds(nx, ny)
    tell(relay.at[0], rounds[0])
    pending = [0]

    def relay_turn():
        r = pending[0]
        if r < len(rounds):
            heard(relay.at[r], rounds[r])
            if r + 1 < len(rounds):
                tell(relay.at[r + 1], rounds[r + 1])
            pending[0] = r + 1

    def turned(t, c):
        tile_copy(t).wait()
        for k in range(slots):
            tiles[t, k] = tiles[t, k].T
        return c

    half = tile_rows // 2
    lax.fori_loop(0, half, turned, 0)
    relay_turn()
    lax.fori_loop(half, tile_rows, turned, 0)
    basis[(steps - 1) * width:, :] = jnp.zeros((width, basis.shape[1]), BF16)
    relay_turn()

    def row_image(j, r):
        acc = jnp.dot(ext[j][tile_cols[r, 0]], tiles[r, 0], preferred_element_type=F32)
        for k in range(1, slots):
            acc = acc + jnp.dot(ext[j][tile_cols[r, k]], tiles[r, k], preferred_element_type=F32)
        return (acc - shifts[j] * ext[j][r].astype(F32)).astype(BF16)

    def own_part():
        return me // stride

    def when_owner(act):
        if stride == 1:
            act()
        else:
            pl.when(lax.rem(me, stride) == 0)(act)

    def rs_copy(u, q):
        p = lax.rem(own_part() + q, parts)
        owner = p * stride
        return owner, pltpu.make_async_remote_copy(
            src_ref=part[u].at[p], dst_ref=landed[u].at[lax.rem(me - owner + count, count) - 1],
            send_sem=rs_send.at[u], recv_sem=rs_recv.at[u],
            device_id=place(owner), device_id_type=MESH)

    def ag_copy(u, d):
        p = own_part()
        return pltpu.make_async_remote_copy(
            src_ref=full[u].at[p], dst_ref=full[u].at[p],
            send_sem=ag_send.at[u], recv_sem=ag_recv.at[u],
            device_id=place(lax.rem(me + d, count)), device_id_type=MESH)

    def scatter(u):
        def send(q, c):
            owner, copy = rs_copy(u, q)
            if stride == 1:
                copy.start()
            else:
                pl.when(owner != me)(copy.start)
            return c
        lax.fori_loop(1 if stride == 1 else 0, parts, send, 0)

    def arrived(ref, sem):
        pltpu.make_async_copy(ref, ref, sem).wait()

    def gather(u):
        def act():
            arrived(landed[u], rs_recv.at[u])
            full[u][own_part()] = (jnp.sum(landed[u][...], axis=0) + part[u][own_part()]) / total

            def send(d, c):
                ag_copy(u, d).start()
                return c
            lax.fori_loop(1, count, send, 0)
        when_owner(act)

    def but_own(act_all, act_rest):
        if stride == 1:
            act_rest()
        else:
            own = lax.rem(me, stride) == 0
            pl.when(own)(act_rest)
            pl.when(jnp.logical_not(own))(act_all)

    def collect(u):
        but_own(lambda: arrived(full[u], ag_recv.at[u]),
                lambda: arrived(full[u].at[:parts - 1], ag_recv.at[u]))

    def drain(u):
        but_own(lambda: arrived(part[u], rs_send.at[u]),
                lambda: arrived(part[u].at[:parts - 1], rs_send.at[u]))
        when_owner(lambda: arrived(landed[u], ag_send.at[u]))

    def column(u, c):
        low = c * per_column
        return jnp.concatenate([full[u][p] for p in range(low, low + per_column)], axis=0)

    def load_part(u, blocks):
        for c, block in enumerate(blocks):
            for a in range(per_column):
                part[u][c * per_column + a] = block[a * PIECE:(a + 1) * PIECE]

    def basis_copy(j):
        rows = slice(j * width, (j + 1) * width)
        return pltpu.make_async_copy(basis.at[rows], basis_out.at[rows], out_sem.at[j])

    for j in range(steps):
        halo_wait(j)
        if j + 1 < steps:
            for s in range(ghosts):
                outbox[j + 1][s] = row_image(j, send_rows[0, s])
                halo_start(j + 1, s, pairs[:3])
            for s in range(ghosts):
                halo_start(j + 1, s, pairs[3:])

        def row(t, c):
            value = row_image(j, t)
            if j + 1 < steps:
                ext[j + 1][t] = value
            basis[j * width:(j + 1) * width, pl.ds(pl.multiple_of(t * tile, tile), tile)] = value
            return c

        lax.fori_loop(0, tile_rows, row, 0, unroll=8)
        basis_copy(j).start()
        if j == 0:
            relay_turn()
        elif j == 1:
            local = nt(basis[:2 * width, :], basis[:2 * width, :])
            load_part(0, [local[:width], local[width:]])
            for _ in rounds:
                relay_turn()
            scatter(0)
        else:
            local = nt(basis[j * width:(j + 1) * width, :], basis[...])
            load_part(j - 1, [local[:, c * LANES:(c + 1) * LANES] for c in range(span // LANES)])
            scatter(j - 1)
            gather(j - 2)
    above[...] = jnp.zeros(above.shape, F32)
    collect(0)
    extend_inverse(0, width, column(0, 0)[:, :width], above)
    extend_inverse(1, width, column(0, 1), above)
    gather(steps - 2)
    for u in range(1, steps - 2):
        collect(u)
        wide = jnp.concatenate([column(u, c) for c in range(span // LANES)], axis=1)
        extend_inverse(u + 1, width, wide[:, :(u + 2) * width], above)
    done = (steps - 1) * width
    chunk = 2 * tile
    for n in range(basis.shape[1] // chunk):
        cols = slice(n * chunk, (n + 1) * chunk)
        early[:, cols] = split_dot(above[:done, :], basis[:, cols])
    early_copy = pltpu.make_async_copy(early, early_out, early_sem)
    early_copy.start()
    collect(steps - 2)
    for c in range(span // LANES):
        gram[:, c * LANES:(c + 1) * LANES] = column(steps - 2, c)
    early_copy.wait()
    for j in range(steps):
        basis_copy(j).wait()
        halo_drain(j)
    for u in range(sums):
        drain(u)


def factor(block, midway=None):
    width = block.shape[0]
    count = width // 8
    eye_r = lax.broadcasted_iota(jnp.int32, (width, width), 0)
    eye_c = lax.broadcasted_iota(jnp.int32, (width, width), 1)
    work = jnp.concatenate([block, jnp.where(eye_r == eye_c, 1.0, 0.0).astype(F32)], axis=1)
    rows = lax.broadcasted_iota(jnp.int32, (8, 2 * width), 0)
    groups = [work[g * 8:(g + 1) * 8] for g in range(count)]
    done = []
    for g in range(count):
        if midway is not None and g == count // 2:
            midway()
        cols = [
            [jnp.broadcast_to(groups[h][:, g * 8 + r:g * 8 + r + 1], (8, 2 * width)) for h in range(g, count)]
            for r in range(8)
        ]
        pivots = cols[0][0]
        for r in range(8):
            inverse = 1.0 / cols[r][0][r:r + 1]
            if r:
                pivots = jnp.where(rows == r, cols[r][0], pivots)
            for m in range(r + 1, 8):
                share = cols[m][0][r:r + 1] * inverse
                cols[m] = [c - d * share for c, d in zip(cols[m], cols[r])]
            scaled = groups[g][r:r + 1] * inverse
            for h in range(g, count):
                update = groups[h] - cols[r][h - g] * scaled
                groups[h] = jnp.where(rows > r, update, groups[h]) if h == g else update
        done.append(groups[g] * lax.rsqrt(pivots))
    return jnp.concatenate(done, axis=0)[:, width:]


def extend_inverse(j, width, gram_row, inverse, midway=None):
    high = lax.Precision.HIGHEST
    lo, hi = j * width, (j + 1) * width
    block = gram_row[:, lo:hi]
    if j:
        previous = inverse[0:lo, 0:lo]
        left = nt(gram_row[:, 0:lo], previous, high)
        block = block - nt(left, left, high)
    own = factor(block, midway)
    inverse[lo:hi, lo:hi] = own
    if j:
        cross = jnp.dot(left, previous, precision=high, preferred_element_type=F32)
        inverse[lo:hi, 0:lo] = -jnp.dot(own, cross, precision=high, preferred_element_type=F32)


def finish_kernel(dims, basis_hbm, early_hbm, gram, above, out, inverse, basis, early, staged, sem):
    steps, width, chunk = dims
    done = (steps - 1) * width
    early_in = pltpu.make_async_copy(early_hbm, early, sem.at[0])
    early_in.start()
    basis_copy = pltpu.make_async_copy(basis_hbm, basis, sem.at[1])
    basis_copy.start()
    early_copy = pltpu.make_async_copy(early, out.at[:done], sem.at[2])

    def pass_on():
        early_in.wait()
        early_copy.start()

    inverse[:done] = above[...]
    extend_inverse(steps - 1, width, gram[...], inverse, pass_on)
    basis_copy.wait()
    copies = []
    for n in range(basis.shape[1] // chunk):
        cols = slice(n * chunk, (n + 1) * chunk)
        staged[:, cols] = split_dot(inverse[done:, :], basis[:, cols])
        copy = pltpu.make_async_copy(staged.at[:, cols], out.at[done:, cols], sem.at[3 + n])
        copy.start()
        copies.append(copy)
    early_copy.wait()
    for copy in copies:
        copy.wait()


def body(nx, ny, start_block, tiles, tile_cols, send_rows, shifts):
    width, nodes = start_block.shape
    tile_rows, slots, tile, _ = tiles.shape
    ghosts = send_rows.shape[1]
    steps = shifts.shape[0]
    size = steps * width
    done = size - width
    sums = steps - 1
    span = -(-size // LANES) * LANES
    parts = (width // PIECE) * (span // LANES)
    count = nx * ny
    dims = (nx, ny, steps, tile_rows, slots, ghosts, tile, width, nodes * count)
    dma = pltpu.SemaphoreType.DMA
    vmem = pl.BlockSpec(memory_space=pltpu.VMEM)
    smem = pl.BlockSpec(memory_space=pltpu.SMEM)
    hbm = pl.BlockSpec(memory_space=pl.ANY)
    basis, early, gram, above = pl.pallas_call(
        functools.partial(krylov_kernel, dims),
        out_shape=(
            jax.ShapeDtypeStruct((size, nodes), BF16),
            jax.ShapeDtypeStruct((done, nodes), F32),
            jax.ShapeDtypeStruct((width, span), F32),
            jax.ShapeDtypeStruct((done, size), F32),
        ),
        in_specs=[smem, smem, smem, vmem, hbm],
        out_specs=(hbm, hbm, vmem, vmem),
        scratch_shapes=[
            pltpu.VMEM(tiles.shape, BF16),
            pltpu.VMEM((size, nodes), BF16),
            pltpu.VMEM((done, nodes), F32),
            pltpu.VMEM((tile_rows, width, tile), BF16),
            dma((tile_rows,)), dma((steps,)), dma,
            dma((steps, ghosts, 4)), dma((steps, ghosts, 4)),
            pltpu.SemaphoreType.REGULAR((len(relay_rounds(nx, ny)),)),
            dma((sums,)), dma((sums,)), dma((sums,)), dma((sums,)),
        ]
        + [pltpu.VMEM((tile_rows + 4 * ghosts, width, tile), BF16) for _ in range(steps)]
        + [pltpu.VMEM((ghosts, width, tile), BF16) for _ in range(steps)]
        + [pltpu.VMEM((parts, PIECE, LANES), F32) for _ in range(sums)]
        + [pltpu.VMEM((count - 1, PIECE, LANES), F32) for _ in range(sums)]
        + [pltpu.VMEM((parts, PIECE, LANES), F32) for _ in range(sums)],
        compiler_params=pltpu.CompilerParams(collective_id=0, has_side_effects=True, vmem_limit_bytes=56 * 2**20),
    )(send_rows, tile_cols, shifts, start_block, tiles)
    chunk = 2 * tile
    return pl.pallas_call(
        functools.partial(finish_kernel, (steps, width, chunk)),
        out_shape=jax.ShapeDtypeStruct((size, nodes), F32),
        in_specs=[hbm, hbm, vmem, vmem],
        out_specs=hbm,
        scratch_shapes=[
            pltpu.VMEM((size, size), F32),
            pltpu.VMEM((size, nodes), BF16),
            pltpu.VMEM((done, nodes), F32),
            pltpu.VMEM((width, nodes), F32),
            dma((3 + nodes // chunk,)),
        ],
        compiler_params=pltpu.CompilerParams(vmem_limit_bytes=56 * 2**20),
    )(basis, early, gram, above)


def solution(mesh):
    in_specs = (
        P(None, ("gx", "gy")),
        P(("gx", "gy"), None, None, None),
        P(("gx", "gy"), None),
        P(("gx", "gy"), None),
        P(),
    )
    out_specs = P(None, ("gx", "gy"))
    run = functools.partial(body, mesh.shape["gx"], mesh.shape["gy"])
    return jax.shard_map(run, mesh=mesh, in_specs=in_specs, out_specs=out_specs, check_vma=False)
```

```python
import functools

import jax
import jax.numpy as jnp
from jax import lax
from jax.experimental import pallas as pl
from jax.experimental.pallas import tpu as pltpu
from jax.sharding import PartitionSpec as P

MESH = pl.DeviceIdType.MESH
F32 = jnp.float32
BF16 = jnp.bfloat16
NT_DIMS = (((1,), (1,)), ((), ()))
LANES = 128
PIECE = 4


def nt(a, b, precision=None):
    return lax.dot_general(a, b, NT_DIMS, precision=precision, preferred_element_type=F32)


def split_dot(left, right):
    rows = left.shape[0]
    main = left.astype(BF16)
    rest = (left - main.astype(F32)).astype(BF16)
    both = jnp.dot(jnp.concatenate([main, rest], axis=0), right, preferred_element_type=F32)
    return both[:rows] + both[rows:]


def relay_rounds(nx, ny):
    rounds = []
    d = 1
    while d < max(nx, ny):
        near = [(0, d), (0, -d)] if d < ny else []
        near += [(d, 0), (-d, 0)] if d < nx else []
        rounds.append(near)
        d *= 2
    rounds.append([(s * d, 0) for d in range(1, nx) for s in (1, -1)])
    return rounds


def krylov_kernel(dims, send_rows, tile_cols, shifts, start, tiles_hbm, basis_out, early_out, gram_out, above_out, *scratch):
    nx, ny, steps, tile_rows, slots, ghosts, tile, width, total = dims
    sums = steps - 1
    size = steps * width
    count = nx * ny
    span = gram_out.shape[1]
    per_column = width // PIECE
    parts = per_column * (span // LANES)
    stride = count // parts
    (gram, above, tail_sem, tiles, basis, early, first, tile_sem, out_sem, early_sem, halo_send, halo_recv, relay,
     rs_send, rs_recv, ag_send, ag_recv) = scratch[:17]
    ext = scratch[17:17 + steps]
    outbox = scratch[17 + steps:17 + 2 * steps]
    part = scratch[17 + 2 * steps:17 + 2 * steps + sums]
    landed = scratch[17 + 2 * steps + sums:17 + 2 * steps + 2 * sums]
    full = scratch[17 + 2 * steps + 2 * sums:17 + 2 * steps + 3 * sums]
    ix, iy = lax.axis_index("gx"), lax.axis_index("gy")
    me = ix * ny + iy

    def tile_copy(t):
        return pltpu.make_async_copy(tiles_hbm.at[t], tiles.at[t], tile_sem.at[t])

    for t in range(tile_rows):
        tile_copy(t).start()

    def inside(dx, dy):
        x, y = ix + dx, iy + dy
        return (x >= 0) & (x < nx) & (y >= 0) & (y < ny)

    def tell(sem, offsets):
        for dx, dy in offsets:
            @pl.when(inside(dx, dy))
            def _():
                pl.semaphore_signal(sem, inc=1, device_id=(ix + dx, iy + dy), device_id_type=MESH)

    def heard(sem, offsets):
        pl.semaphore_wait(sem, sum(jnp.where(inside(dx, dy), 1, 0) for dx, dy in offsets))

    sides = [(0, 1), (0, -1), (1, 0), (-1, 0)]
    slot_of = {(1, 0): 0, (-1, 0): 1, (0, 1): 2, (0, -1): 3}
    barrier = pltpu.get_barrier_semaphore()
    tell(barrier, sides)

    for t in range(tile_rows):
        rows = start[:, t * tile:(t + 1) * tile]
        ext[0][t] = rows
        first[t] = rows
    for s in range(ghosts):
        outbox[0][s] = first[send_rows[0, s]]

    def edges(j):
        for dx, dy in sides:
            low = tile_rows + slot_of[dx, dy] * ghosts

            @pl.when(jnp.logical_not(inside(-dx, -dy)))
            def _():
                ext[j][low:low + ghosts] = jnp.zeros((ghosts, width, tile), BF16)

    for j in range(steps):
        edges(j)
    heard(barrier, sides)

    far = jnp.where(lax.rem(ix, 2) == 1, 1, -1)
    far_pair = (far, 0, jnp.where(far == 1, 0, 1), jnp.where(far == 1, 1, 0), 0)
    near_pair = (-far, 0, jnp.where(far == 1, 1, 0), jnp.where(far == 1, 0, 1), 1)
    up_pair = (0, 1, 2, 2, 2)
    down_pair = (0, -1, 3, 3, 3)
    pairs = (far_pair, up_pair, down_pair, near_pair)

    def halo(j, s, pair, incoming=False):
        dx, dy, lands, comes, n = pair
        return pltpu.make_async_remote_copy(
            src_ref=outbox[j].at[s],
            dst_ref=ext[j].at[tile_rows + (comes if incoming else lands) * ghosts + s],
            send_sem=halo_send.at[j, s, n], recv_sem=halo_recv.at[j, s, n],
            device_id=(ix + dx, iy + dy), device_id_type=MESH)

    def halo_start(j, s, some):
        for pair in some:
            @pl.when(inside(pair[0], pair[1]))
            def _():
                halo(j, s, pair).start()

    def halo_wait(j):
        for pair in pairs:
            back = 1 if pair[1] == 0 else -1

            @pl.when(inside(pair[0], back * pair[1]))
            def _():
                for s in range(ghosts):
                    halo(j, s, pair, True).wait_recv()

    def halo_drain(j):
        for pair in pairs:
            @pl.when(inside(pair[0], pair[1]))
            def _():
                for s in range(ghosts):
                    halo(j, s, pair).wait_send()

    for s in range(ghosts):
        halo_start(0, s, pairs[:1])
    for s in range(ghosts):
        halo_start(0, s, pairs[1:])

    rounds = relay_rounds(nx, ny)
    tell(relay.at[0], rounds[0])
    pending = [0]

    def relay_turn():
        r = pending[0]
        if r < len(rounds):
            heard(relay.at[r], rounds[r])
            if r + 1 < len(rounds):
                tell(relay.at[r + 1], rounds[r + 1])
            pending[0] = r + 1

    def turned(t, c):
        tile_copy(t).wait()
        for k in range(slots):
            tiles[t, k] = tiles[t, k].T
        return c

    half = tile_rows // 2
    lax.fori_loop(0, half, turned, 0)
    relay_turn()
    lax.fori_loop(half, tile_rows, turned, 0)
    basis[(steps - 1) * width:, :] = jnp.zeros((width, basis.shape[1]), BF16)
    relay_turn()

    def row_image(j, r):
        acc = jnp.dot(ext[j][tile_cols[r, 0]], tiles[r, 0], preferred_element_type=F32)
        for k in range(1, slots):
            acc = acc + jnp.dot(ext[j][tile_cols[r, k]], tiles[r, k], preferred_element_type=F32)
        return (acc - shifts[j] * ext[j][r].astype(F32)).astype(BF16)

    def own_part():
        return me // stride

    def when_owner(act):
        if stride == 1:
            act()
        else:
            pl.when(lax.rem(me, stride) == 0)(act)

    def wrap(i, n):
        return jnp.where(i >= n, i - n, i)

    def each_other(act):
        for a in range(nx):
            x = wrap(ix + a, nx)

            def turn(b, c):
                act(x, wrap(iy + b, ny), a * ny + b - 1)
                return c
            lax.fori_loop(0 if a else 1, ny, turn, 0, unroll=4)

    def scatter(u):
        def send(x, y, slot):
            owner = x * ny + y

            def go():
                pltpu.make_async_remote_copy(
                    src_ref=part[u].at[owner // stride], dst_ref=landed[u].at[slot],
                    send_sem=rs_send.at[u], recv_sem=rs_recv.at[u],
                    device_id=(x, y), device_id_type=MESH).start()
            if stride == 1:
                go()
            else:
                pl.when(lax.rem(owner, stride) == 0)(go)
        each_other(send)

    def announce(u):
        p = own_part()

        def send(x, y, slot):
            pltpu.make_async_remote_copy(
                src_ref=full[u].at[p], dst_ref=full[u].at[p],
                send_sem=ag_send.at[u], recv_sem=ag_recv.at[u],
                device_id=(x, y), device_id_type=MESH).start()
        each_other(send)

    def arrived(ref, sem):
        pltpu.make_async_copy(ref, ref, sem).wait()

    def gather(u):
        def act():
            arrived(landed[u], rs_recv.at[u])
            full[u][own_part()] = (jnp.sum(landed[u][...], axis=0) + part[u][own_part()]) / total
            announce(u)
        when_owner(act)

    def but_own(act_all, act_rest):
        if stride == 1:
            act_rest()
        else:
            own = lax.rem(me, stride) == 0
            pl.when(own)(act_rest)
            pl.when(jnp.logical_not(own))(act_all)

    def collect(u):
        but_own(lambda: arrived(full[u], ag_recv.at[u]),
                lambda: arrived(full[u].at[:parts - 1], ag_recv.at[u]))

    def drain_scatter(u):
        but_own(lambda: arrived(part[u], rs_send.at[u]),
                lambda: arrived(part[u].at[:parts - 1], rs_send.at[u]))

    def drain_gather(u):
        when_owner(lambda: arrived(landed[u], ag_send.at[u]))

    def column(u, c):
        low = c * per_column
        return jnp.concatenate([full[u][p] for p in range(low, low + per_column)], axis=0)

    def load_part(u, blocks):
        for c, block in enumerate(blocks):
            for a in range(per_column):
                part[u][c * per_column + a] = block[a * PIECE:(a + 1) * PIECE]

    def basis_copy(j):
        rows = slice(j * width, (j + 1) * width)
        return pltpu.make_async_copy(basis.at[rows], basis_out.at[rows], out_sem.at[j])

    for j in range(steps):
        halo_wait(j)
        if j + 1 < steps:
            for s in range(ghosts):
                outbox[j + 1][s] = row_image(j, send_rows[0, s])
                halo_start(j + 1, s, pairs[:3])
            for s in range(ghosts):
                halo_start(j + 1, s, pairs[3:])

        def row(t, c):
            value = row_image(j, t)
            if j + 1 < steps:
                ext[j + 1][t] = value
            cols = pl.ds(pl.multiple_of(t * tile, tile), tile)
            basis[j * width:(j + 1) * width, cols] = value
            if j + 1 == steps:
                c = c + nt(value, basis[:, cols])
            return c

        carry = jnp.zeros((width, size), F32) if j + 1 == steps else 0
        carry = lax.fori_loop(0, tile_rows, row, carry, unroll=8)
        basis_copy(j).start()
        if j == 0:
            relay_turn()
        elif j == 1:
            local = nt(basis[:2 * width, :], basis[:2 * width, :])
            load_part(0, [local[:width], local[width:]])
            for _ in rounds:
                relay_turn()
            scatter(0)
        else:
            local = carry if j + 1 == steps else nt(basis[j * width:(j + 1) * width, :], basis[...])
            load_part(j - 1, [local[:, c * LANES:(c + 1) * LANES] for c in range(span // LANES)])
            scatter(j - 1)
            gather(j - 2)
    above[...] = jnp.zeros(above.shape, F32)
    collect(0)
    extend_inverse(0, width, column(0, 0)[:, :width], above)
    extend_inverse(1, width, column(0, 1), above)
    gather(steps - 2)
    for u in range(1, steps - 2):
        collect(u)
        wide = jnp.concatenate([column(u, c) for c in range(span // LANES)], axis=1)
        extend_inverse(u + 1, width, wide[:, :(u + 2) * width], above)
    above_copy = pltpu.make_async_copy(above, above_out, tail_sem.at[0])
    above_copy.start()
    done = (steps - 1) * width
    chunk = 2 * tile
    for n in range(basis.shape[1] // chunk):
        cols = slice(n * chunk, (n + 1) * chunk)
        early[:, cols] = split_dot(above[:done, :], basis[:, cols])
    early_copy = pltpu.make_async_copy(early, early_out, early_sem)
    early_copy.start()
    for j in range(steps):
        basis_copy(j).wait()
        halo_drain(j)
    for u in range(sums):
        drain_scatter(u)
        if u + 1 < sums:
            drain_gather(u)
    above_copy.wait()
    collect(sums - 1)
    for c in range(span // LANES):
        gram[:, c * LANES:(c + 1) * LANES] = column(sums - 1, c)
    gram_copy = pltpu.make_async_copy(gram, gram_out, tail_sem.at[1])
    gram_copy.start()
    drain_gather(sums - 1)
    early_copy.wait()
    gram_copy.wait()


def factor(block, midway=None):
    width = block.shape[0]
    count = width // 8
    eye_r = lax.broadcasted_iota(jnp.int32, (width, width), 0)
    eye_c = lax.broadcasted_iota(jnp.int32, (width, width), 1)
    work = jnp.concatenate([block, jnp.where(eye_r == eye_c, 1.0, 0.0).astype(F32)], axis=1)
    rows = lax.broadcasted_iota(jnp.int32, (8, 2 * width), 0)
    groups = [work[g * 8:(g + 1) * 8] for g in range(count)]
    done = []
    for g in range(count):
        if midway is not None and g == count // 2:
            midway()
        cols = [
            [jnp.broadcast_to(groups[h][:, g * 8 + r:g * 8 + r + 1], (8, 2 * width)) for h in range(g, count)]
            for r in range(8)
        ]
        pivots = cols[0][0]
        for r in range(8):
            inverse = 1.0 / cols[r][0][r:r + 1]
            if r:
                pivots = jnp.where(rows == r, cols[r][0], pivots)
            for m in range(r + 1, 8):
                share = cols[m][0][r:r + 1] * inverse
                cols[m] = [c - d * share for c, d in zip(cols[m], cols[r])]
            scaled = groups[g][r:r + 1] * inverse
            for h in range(g, count):
                update = groups[h] - cols[r][h - g] * scaled
                groups[h] = jnp.where(rows > r, update, groups[h]) if h == g else update
        done.append(groups[g] * lax.rsqrt(pivots))
    return jnp.concatenate(done, axis=0)[:, width:]


def extend_inverse(j, width, gram_row, inverse, midway=None):
    high = lax.Precision.HIGHEST
    lo, hi = j * width, (j + 1) * width
    block = gram_row[:, lo:hi]
    if j:
        previous = inverse[0:lo, 0:lo]
        left = nt(gram_row[:, 0:lo], previous, high)
        block = block - nt(left, left, high)
    own = factor(block, midway)
    inverse[lo:hi, lo:hi] = own
    if j:
        cross = jnp.dot(left, previous, precision=high, preferred_element_type=F32)
        inverse[lo:hi, 0:lo] = -jnp.dot(own, cross, precision=high, preferred_element_type=F32)


def finish_kernel(dims, basis_hbm, early_hbm, gram_hbm, above_hbm, out, gram, inverse, basis, early, staged, sem):
    steps, width, chunk = dims
    done = (steps - 1) * width
    gram_in = pltpu.make_async_copy(gram_hbm, gram, sem.at[3])
    above_in = pltpu.make_async_copy(above_hbm, inverse.at[:done], sem.at[4])
    early_in = pltpu.make_async_copy(early_hbm, early, sem.at[0])
    basis_copy = pltpu.make_async_copy(basis_hbm, basis, sem.at[1])
    for copy in (gram_in, above_in, early_in, basis_copy):
        copy.start()
    early_copy = pltpu.make_async_copy(early, out.at[:done], sem.at[2])

    def pass_on():
        early_in.wait()
        early_copy.start()

    gram_in.wait()
    above_in.wait()
    extend_inverse(steps - 1, width, gram[...], inverse, pass_on)
    basis_copy.wait()
    copies = []
    for n in range(basis.shape[1] // chunk):
        cols = slice(n * chunk, (n + 1) * chunk)
        staged[:, cols] = split_dot(inverse[done:, :], basis[:, cols])
        copy = pltpu.make_async_copy(staged.at[:, cols], out.at[done:, cols], sem.at[5 + n])
        copy.start()
        copies.append(copy)
    early_copy.wait()
    for copy in copies:
        copy.wait()


def body(nx, ny, start_block, tiles, tile_cols, send_rows, shifts):
    width, nodes = start_block.shape
    tile_rows, slots, tile, _ = tiles.shape
    ghosts = send_rows.shape[1]
    steps = shifts.shape[0]
    size = steps * width
    done = size - width
    sums = steps - 1
    span = -(-size // LANES) * LANES
    parts = (width // PIECE) * (span // LANES)
    count = nx * ny
    dims = (nx, ny, steps, tile_rows, slots, ghosts, tile, width, nodes * count)
    dma = pltpu.SemaphoreType.DMA
    vmem = pl.BlockSpec(memory_space=pltpu.VMEM)
    smem = pl.BlockSpec(memory_space=pltpu.SMEM)
    hbm = pl.BlockSpec(memory_space=pl.ANY)
    basis, early, gram, above = pl.pallas_call(
        functools.partial(krylov_kernel, dims),
        out_shape=(
            jax.ShapeDtypeStruct((size, nodes), BF16),
            jax.ShapeDtypeStruct((done, nodes), F32),
            jax.ShapeDtypeStruct((width, span), F32),
            jax.ShapeDtypeStruct((done, size), F32),
        ),
        in_specs=[smem, smem, smem, vmem, hbm],
        out_specs=(hbm, hbm, hbm, hbm),
        scratch_shapes=[
            pltpu.VMEM((width, span), F32),
            pltpu.VMEM((done, size), F32),
            dma((2,)),
            pltpu.VMEM(tiles.shape, BF16),
            pltpu.VMEM((size, nodes), BF16),
            pltpu.VMEM((done, nodes), F32),
            pltpu.VMEM((tile_rows, width, tile), BF16),
            dma((tile_rows,)), dma((steps,)), dma,
            dma((steps, ghosts, 4)), dma((steps, ghosts, 4)),
            pltpu.SemaphoreType.REGULAR((len(relay_rounds(nx, ny)),)),
            dma((sums,)), dma((sums,)), dma((sums,)), dma((sums,)),
        ]
        + [pltpu.VMEM((tile_rows + 4 * ghosts, width, tile), BF16) for _ in range(steps)]
        + [pltpu.VMEM((ghosts, width, tile), BF16) for _ in range(steps)]
        + [pltpu.VMEM((parts, PIECE, LANES), F32) for _ in range(sums)]
        + [pltpu.VMEM((count - 1, PIECE, LANES), F32) for _ in range(sums)]
        + [pltpu.VMEM((parts, PIECE, LANES), F32) for _ in range(sums)],
        compiler_params=pltpu.CompilerParams(collective_id=0, has_side_effects=True, vmem_limit_bytes=56 * 2**20),
    )(send_rows, tile_cols, shifts, start_block, tiles)
    chunk = 2 * tile
    return pl.pallas_call(
        functools.partial(finish_kernel, (steps, width, chunk)),
        out_shape=jax.ShapeDtypeStruct((size, nodes), F32),
        in_specs=[hbm, hbm, hbm, hbm],
        out_specs=hbm,
        scratch_shapes=[
            pltpu.VMEM((width, span), F32),
            pltpu.VMEM((size, size), F32),
            pltpu.VMEM((size, nodes), BF16),
            pltpu.VMEM((done, nodes), F32),
            pltpu.VMEM((width, nodes), F32),
            dma((5 + nodes // chunk,)),
        ],
        compiler_params=pltpu.CompilerParams(vmem_limit_bytes=56 * 2**20),
    )(basis, early, gram, above)


def solution(mesh):
    in_specs = (
        P(None, ("gx", "gy")),
        P(("gx", "gy"), None, None, None),
        P(("gx", "gy"), None),
        P(("gx", "gy"), None),
        P(),
    )
    out_specs = P(None, ("gx", "gy"))
    run = functools.partial(body, mesh.shape["gx"], mesh.shape["gy"])
    return jax.shard_map(run, mesh=mesh, in_specs=in_specs, out_specs=out_specs, check_vma=False)
```

```python
import functools

import jax
import jax.numpy as jnp
from jax import lax
from jax.experimental import pallas as pl
from jax.experimental.pallas import tpu as pltpu
from jax.sharding import PartitionSpec as P

MESH = pl.DeviceIdType.MESH
F32 = jnp.float32
BF16 = jnp.bfloat16
NT_DIMS = (((1,), (1,)), ((), ()))
LANES = 128
PIECE = 4


def nt(a, b, precision=None):
    return lax.dot_general(a, b, NT_DIMS, precision=precision, preferred_element_type=F32)


def split_dot(left, right):
    rows = left.shape[0]
    main = left.astype(BF16)
    rest = (left - main.astype(F32)).astype(BF16)
    both = jnp.dot(jnp.concatenate([main, rest], axis=0), right, preferred_element_type=F32)
    return both[:rows] + both[rows:]


def relay_rounds(nx, ny):
    rounds = []
    d = 1
    while d < max(nx, ny):
        near = [(0, d), (0, -d)] if d < ny else []
        near += [(d, 0), (-d, 0)] if d < nx else []
        rounds.append(near)
        d *= 2
    rounds.append([(s * d, 0) for d in range(1, nx) for s in (1, -1)])
    return rounds


def krylov_kernel(dims, send_rows_hbm, tile_cols_hbm, shifts_hbm, start_hbm, tiles_hbm, basis_out, early_out, gram_out, above_out, *scratch):
    nx, ny, steps, tile_rows, slots, ghosts, tile, width, total = dims
    sums = steps - 1
    size = steps * width
    count = nx * ny
    span = gram_out.shape[1]
    per_column = width // PIECE
    parts = per_column * (span // LANES)
    stride = count // parts
    (send_rows, tile_cols, shifts, small_sem, gram, above, tail_sem, tiles, basis, early, first, tile_sem, out_sem, early_sem, halo_send, halo_recv, relay,
     rs_send, rs_recv, ag_send, ag_recv) = scratch[:21]
    ext = scratch[21:21 + steps]
    outbox = scratch[21 + steps:21 + 2 * steps]
    part = scratch[21 + 2 * steps:21 + 2 * steps + sums]
    landed = scratch[21 + 2 * steps + sums:21 + 2 * steps + 2 * sums]
    full = scratch[21 + 2 * steps + 2 * sums:21 + 2 * steps + 3 * sums]
    ix, iy = lax.axis_index("gx"), lax.axis_index("gy")
    me = ix * ny + iy

    def inside(dx, dy):
        x, y = ix + dx, iy + dy
        return (x >= 0) & (x < nx) & (y >= 0) & (y < ny)

    def tell(sem, offsets):
        for dx, dy in offsets:
            @pl.when(inside(dx, dy))
            def _():
                pl.semaphore_signal(sem, inc=1, device_id=(ix + dx, iy + dy), device_id_type=MESH)

    def heard(sem, offsets):
        pl.semaphore_wait(sem, sum(jnp.where(inside(dx, dy), 1, 0) for dx, dy in offsets))

    sides = [(0, 1), (0, -1), (1, 0), (-1, 0)]
    slot_of = {(1, 0): 0, (-1, 0): 1, (0, 1): 2, (0, -1): 3}
    barrier = pltpu.get_barrier_semaphore()
    tell(barrier, sides)

    small = [
        pltpu.make_async_copy(send_rows_hbm, send_rows, small_sem.at[0]),
        pltpu.make_async_copy(tile_cols_hbm, tile_cols, small_sem.at[1]),
        pltpu.make_async_copy(shifts_hbm, shifts, small_sem.at[2]),
    ]
    for t in range(tile_rows):
        small.append(pltpu.make_async_copy(start_hbm.at[:, t * tile:(t + 1) * tile], first.at[t], small_sem.at[3 + t]))
    for copy in small:
        copy.start()

    def tile_copy(t):
        return pltpu.make_async_copy(tiles_hbm.at[t], tiles.at[t], tile_sem.at[t])

    for t in range(tile_rows):
        tile_copy(t).start()


    def edges(j):
        for dx, dy in sides:
            low = tile_rows + slot_of[dx, dy] * ghosts

            @pl.when(jnp.logical_not(inside(-dx, -dy)))
            def _():
                ext[j][low:low + ghosts] = jnp.zeros((ghosts, width, tile), BF16)

    for j in range(steps):
        edges(j)
    for copy in small:
        copy.wait()
    for s in range(ghosts):
        outbox[0][s] = first[send_rows[0, s]]
    heard(barrier, sides)

    far = jnp.where(lax.rem(ix, 2) == 1, 1, -1)
    far_pair = (far, 0, jnp.where(far == 1, 0, 1), jnp.where(far == 1, 1, 0), 0)
    near_pair = (-far, 0, jnp.where(far == 1, 1, 0), jnp.where(far == 1, 0, 1), 1)
    up_pair = (0, 1, 2, 2, 2)
    down_pair = (0, -1, 3, 3, 3)
    pairs = (far_pair, up_pair, down_pair, near_pair)

    def halo(j, s, pair, incoming=False):
        dx, dy, lands, comes, n = pair
        return pltpu.make_async_remote_copy(
            src_ref=outbox[j].at[s],
            dst_ref=ext[j].at[tile_rows + (comes if incoming else lands) * ghosts + s],
            send_sem=halo_send.at[j, s, n], recv_sem=halo_recv.at[j, s, n],
            device_id=(ix + dx, iy + dy), device_id_type=MESH)

    def halo_start(j, s, some):
        for pair in some:
            @pl.when(inside(pair[0], pair[1]))
            def _():
                halo(j, s, pair).start()

    def halo_wait(j):
        for pair in pairs:
            back = 1 if pair[1] == 0 else -1

            @pl.when(inside(pair[0], back * pair[1]))
            def _():
                for s in range(ghosts):
                    halo(j, s, pair, True).wait_recv()

    def halo_drain(j):
        for pair in pairs:
            @pl.when(inside(pair[0], pair[1]))
            def _():
                for s in range(ghosts):
                    halo(j, s, pair).wait_send()

    for s in range(ghosts):
        halo_start(0, s, pairs[:1])
    for s in range(ghosts):
        halo_start(0, s, pairs[1:])

    ext[0][:tile_rows] = first[...]
    rounds = relay_rounds(nx, ny)
    tell(relay.at[0], rounds[0])
    pending = [0]

    def relay_turn():
        r = pending[0]
        if r < len(rounds):
            heard(relay.at[r], rounds[r])
            if r + 1 < len(rounds):
                tell(relay.at[r + 1], rounds[r + 1])
            pending[0] = r + 1

    def turned(t, c):
        tile_copy(t).wait()
        for k in range(slots):
            tiles[t, k] = tiles[t, k].T
        return c

    half = tile_rows // 2
    lax.fori_loop(0, half, turned, 0)
    relay_turn()
    lax.fori_loop(half, tile_rows, turned, 0)
    basis[(steps - 1) * width:, :] = jnp.zeros((width, basis.shape[1]), BF16)
    relay_turn()

    def row_image(j, r):
        acc = jnp.dot(ext[j][tile_cols[r, 0]], tiles[r, 0], preferred_element_type=F32)
        for k in range(1, slots):
            acc = acc + jnp.dot(ext[j][tile_cols[r, k]], tiles[r, k], preferred_element_type=F32)
        return (acc - shifts[j] * ext[j][r].astype(F32)).astype(BF16)

    def own_part():
        return me // stride

    def when_owner(act):
        if stride == 1:
            act()
        else:
            pl.when(lax.rem(me, stride) == 0)(act)

    def wrap(i, n):
        return jnp.where(i >= n, i - n, i)

    def each_other(act):
        for a in range(nx):
            x = wrap(ix + a, nx)

            def turn(b, c):
                act(x, wrap(iy + b, ny), a * ny + b - 1)
                return c
            lax.fori_loop(0 if a else 1, ny, turn, 0, unroll=4)

    def scatter(u):
        def send(x, y, slot):
            owner = x * ny + y

            def go():
                pltpu.make_async_remote_copy(
                    src_ref=part[u].at[owner // stride], dst_ref=landed[u].at[slot],
                    send_sem=rs_send.at[u], recv_sem=rs_recv.at[u],
                    device_id=(x, y), device_id_type=MESH).start()
            if stride == 1:
                go()
            else:
                pl.when(lax.rem(owner, stride) == 0)(go)
        each_other(send)

    def announce(u):
        p = own_part()

        def send(x, y, slot):
            pltpu.make_async_remote_copy(
                src_ref=full[u].at[p], dst_ref=full[u].at[p],
                send_sem=ag_send.at[u], recv_sem=ag_recv.at[u],
                device_id=(x, y), device_id_type=MESH).start()
        each_other(send)

    def arrived(ref, sem):
        pltpu.make_async_copy(ref, ref, sem).wait()

    def gather(u):
        def act():
            arrived(landed[u], rs_recv.at[u])
            full[u][own_part()] = (jnp.sum(landed[u][...], axis=0) + part[u][own_part()]) / total
            announce(u)
        when_owner(act)

    def but_own(act_all, act_rest):
        if stride == 1:
            act_rest()
        else:
            own = lax.rem(me, stride) == 0
            pl.when(own)(act_rest)
            pl.when(jnp.logical_not(own))(act_all)

    def collect(u):
        but_own(lambda: arrived(full[u], ag_recv.at[u]),
                lambda: arrived(full[u].at[:parts - 1], ag_recv.at[u]))

    def drain_scatter(u):
        but_own(lambda: arrived(part[u], rs_send.at[u]),
                lambda: arrived(part[u].at[:parts - 1], rs_send.at[u]))

    def drain_gather(u):
        when_owner(lambda: arrived(landed[u], ag_send.at[u]))

    def column(u, c):
        low = c * per_column
        return jnp.concatenate([full[u][p] for p in range(low, low + per_column)], axis=0)

    def load_part(u, blocks):
        for c, block in enumerate(blocks):
            for a in range(per_column):
                part[u][c * per_column + a] = block[a * PIECE:(a + 1) * PIECE]

    def basis_copy(j):
        rows = slice(j * width, (j + 1) * width)
        return pltpu.make_async_copy(basis.at[rows], basis_out.at[rows], out_sem.at[j])

    for j in range(steps):
        halo_wait(j)
        if j + 1 < steps:
            for s in range(ghosts):
                outbox[j + 1][s] = row_image(j, send_rows[0, s])
                halo_start(j + 1, s, pairs[:3])
            for s in range(ghosts):
                halo_start(j + 1, s, pairs[3:])

        def row(t, c):
            value = row_image(j, t)
            if j + 1 < steps:
                ext[j + 1][t] = value
            cols = pl.ds(pl.multiple_of(t * tile, tile), tile)
            basis[j * width:(j + 1) * width, cols] = value
            if j + 1 == steps:
                c = c + nt(value, basis[:, cols])
            return c

        carry = jnp.zeros((width, size), F32) if j + 1 == steps else 0
        carry = lax.fori_loop(0, tile_rows, row, carry, unroll=8)
        basis_copy(j).start()
        if j == 0:
            relay_turn()
        elif j == 1:
            local = nt(basis[:2 * width, :], basis[:2 * width, :])
            load_part(0, [local[:width], local[width:]])
            for _ in rounds:
                relay_turn()
            scatter(0)
        else:
            local = carry if j + 1 == steps else nt(basis[j * width:(j + 1) * width, :], basis[...])
            load_part(j - 1, [local[:, c * LANES:(c + 1) * LANES] for c in range(span // LANES)])
            scatter(j - 1)
            gather(j - 2)
    above[...] = jnp.zeros(above.shape, F32)
    collect(0)
    extend_inverse(0, width, column(0, 0)[:, :width], above)
    extend_inverse(1, width, column(0, 1), above)
    gather(steps - 2)
    for u in range(1, steps - 2):
        collect(u)
        wide = jnp.concatenate([column(u, c) for c in range(span // LANES)], axis=1)
        extend_inverse(u + 1, width, wide[:, :(u + 2) * width], above)
    above_copy = pltpu.make_async_copy(above, above_out, tail_sem.at[0])
    above_copy.start()
    done = (steps - 1) * width
    chunk = 2 * tile
    for n in range(basis.shape[1] // chunk):
        cols = slice(n * chunk, (n + 1) * chunk)
        early[:, cols] = split_dot(above[:done, :], basis[:, cols])
    early_copy = pltpu.make_async_copy(early, early_out, early_sem)
    early_copy.start()
    for j in range(steps):
        basis_copy(j).wait()
        halo_drain(j)
    for u in range(sums):
        drain_scatter(u)
        if u + 1 < sums:
            drain_gather(u)
    above_copy.wait()
    collect(sums - 1)
    for c in range(span // LANES):
        gram[:, c * LANES:(c + 1) * LANES] = column(sums - 1, c)
    gram_copy = pltpu.make_async_copy(gram, gram_out, tail_sem.at[1])
    gram_copy.start()
    drain_gather(sums - 1)
    early_copy.wait()
    gram_copy.wait()


def factor(block, midway=None):
    width = block.shape[0]
    count = width // 8
    eye_r = lax.broadcasted_iota(jnp.int32, (width, width), 0)
    eye_c = lax.broadcasted_iota(jnp.int32, (width, width), 1)
    work = jnp.concatenate([block, jnp.where(eye_r == eye_c, 1.0, 0.0).astype(F32)], axis=1)
    rows = lax.broadcasted_iota(jnp.int32, (8, 2 * width), 0)
    groups = [work[g * 8:(g + 1) * 8] for g in range(count)]
    done = []
    for g in range(count):
        if midway is not None and g == count // 2:
            midway()
        cols = [
            [jnp.broadcast_to(groups[h][:, g * 8 + r:g * 8 + r + 1], (8, 2 * width)) for h in range(g, count)]
            for r in range(8)
        ]
        pivots = cols[0][0]
        for r in range(8):
            inverse = 1.0 / cols[r][0][r:r + 1]
            if r:
                pivots = jnp.where(rows == r, cols[r][0], pivots)
            for m in range(r + 1, 8):
                share = cols[m][0][r:r + 1] * inverse
                cols[m] = [c - d * share for c, d in zip(cols[m], cols[r])]
            scaled = groups[g][r:r + 1] * inverse
            for h in range(g, count):
                update = groups[h] - cols[r][h - g] * scaled
                groups[h] = jnp.where(rows > r, update, groups[h]) if h == g else update
        done.append(groups[g] * lax.rsqrt(pivots))
    return jnp.concatenate(done, axis=0)[:, width:]


def extend_inverse(j, width, gram_row, inverse, midway=None):
    high = lax.Precision.HIGHEST
    lo, hi = j * width, (j + 1) * width
    block = gram_row[:, lo:hi]
    if j:
        previous = inverse[0:lo, 0:lo]
        left = nt(gram_row[:, 0:lo], previous, high)
        block = block - nt(left, left, high)
    own = factor(block, midway)
    inverse[lo:hi, lo:hi] = own
    if j:
        cross = jnp.dot(left, previous, precision=high, preferred_element_type=F32)
        inverse[lo:hi, 0:lo] = -jnp.dot(own, cross, precision=high, preferred_element_type=F32)


def finish_kernel(dims, basis_hbm, early_hbm, gram_hbm, above_hbm, out, gram, inverse, basis, early, staged, sem):
    steps, width, chunk = dims
    done = (steps - 1) * width
    gram_in = pltpu.make_async_copy(gram_hbm, gram, sem.at[3])
    above_in = pltpu.make_async_copy(above_hbm, inverse.at[:done], sem.at[4])
    early_in = pltpu.make_async_copy(early_hbm, early, sem.at[0])
    basis_copy = pltpu.make_async_copy(basis_hbm, basis, sem.at[1])
    for copy in (gram_in, above_in, early_in, basis_copy):
        copy.start()
    early_copy = pltpu.make_async_copy(early, out.at[:done], sem.at[2])

    def pass_on():
        early_in.wait()
        early_copy.start()

    gram_in.wait()
    above_in.wait()
    extend_inverse(steps - 1, width, gram[...], inverse, pass_on)
    basis_copy.wait()
    copies = []
    for n in range(basis.shape[1] // chunk):
        cols = slice(n * chunk, (n + 1) * chunk)
        staged[:, cols] = split_dot(inverse[done:, :], basis[:, cols])
        copy = pltpu.make_async_copy(staged.at[:, cols], out.at[done:, cols], sem.at[5 + n])
        copy.start()
        copies.append(copy)
    early_copy.wait()
    for copy in copies:
        copy.wait()


def body(nx, ny, start_block, tiles, tile_cols, send_rows, shifts):
    width, nodes = start_block.shape
    tile_rows, slots, tile, _ = tiles.shape
    ghosts = send_rows.shape[1]
    steps = shifts.shape[0]
    size = steps * width
    done = size - width
    sums = steps - 1
    span = -(-size // LANES) * LANES
    parts = (width // PIECE) * (span // LANES)
    count = nx * ny
    dims = (nx, ny, steps, tile_rows, slots, ghosts, tile, width, nodes * count)
    dma = pltpu.SemaphoreType.DMA
    hbm = pl.BlockSpec(memory_space=pl.ANY)
    basis, early, gram, above = pl.pallas_call(
        functools.partial(krylov_kernel, dims),
        out_shape=(
            jax.ShapeDtypeStruct((size, nodes), BF16),
            jax.ShapeDtypeStruct((done, nodes), F32),
            jax.ShapeDtypeStruct((width, span), F32),
            jax.ShapeDtypeStruct((done, size), F32),
        ),
        in_specs=[hbm] * 5,
        out_specs=(hbm, hbm, hbm, hbm),
        scratch_shapes=[
            pltpu.SMEM(send_rows.shape, jnp.int32),
            pltpu.SMEM(tile_cols.shape, jnp.int32),
            pltpu.SMEM(shifts.shape, F32),
            dma((3 + tile_rows,)),
            pltpu.VMEM((width, span), F32),
            pltpu.VMEM((done, size), F32),
            dma((2,)),
            pltpu.VMEM(tiles.shape, BF16),
            pltpu.VMEM((size, nodes), BF16),
            pltpu.VMEM((done, nodes), F32),
            pltpu.VMEM((tile_rows, width, tile), BF16),
            dma((tile_rows,)), dma((steps,)), dma,
            dma((steps, ghosts, 4)), dma((steps, ghosts, 4)),
            pltpu.SemaphoreType.REGULAR((len(relay_rounds(nx, ny)),)),
            dma((sums,)), dma((sums,)), dma((sums,)), dma((sums,)),
        ]
        + [pltpu.VMEM((tile_rows + 4 * ghosts, width, tile), BF16) for _ in range(steps)]
        + [pltpu.VMEM((ghosts, width, tile), BF16) for _ in range(steps)]
        + [pltpu.VMEM((parts, PIECE, LANES), F32) for _ in range(sums)]
        + [pltpu.VMEM((count - 1, PIECE, LANES), F32) for _ in range(sums)]
        + [pltpu.VMEM((parts, PIECE, LANES), F32) for _ in range(sums)],
        compiler_params=pltpu.CompilerParams(collective_id=0, has_side_effects=True, vmem_limit_bytes=56 * 2**20),
    )(send_rows, tile_cols, shifts, start_block, tiles)
    chunk = 2 * tile
    return pl.pallas_call(
        functools.partial(finish_kernel, (steps, width, chunk)),
        out_shape=jax.ShapeDtypeStruct((size, nodes), F32),
        in_specs=[hbm, hbm, hbm, hbm],
        out_specs=hbm,
        scratch_shapes=[
            pltpu.VMEM((width, span), F32),
            pltpu.VMEM((size, size), F32),
            pltpu.VMEM((size, nodes), BF16),
            pltpu.VMEM((done, nodes), F32),
            pltpu.VMEM((width, nodes), F32),
            dma((5 + nodes // chunk,)),
        ],
        compiler_params=pltpu.CompilerParams(vmem_limit_bytes=56 * 2**20),
    )(basis, early, gram, above)


def solution(mesh):
    in_specs = (
        P(None, ("gx", "gy")),
        P(("gx", "gy"), None, None, None),
        P(("gx", "gy"), None),
        P(("gx", "gy"), None),
        P(),
    )
    out_specs = P(None, ("gx", "gy"))
    run = functools.partial(body, mesh.shape["gx"], mesh.shape["gy"])
    return jax.shard_map(run, mesh=mesh, in_specs=in_specs, out_specs=out_specs, check_vma=False)
```

```python
import functools

import jax
import jax.numpy as jnp
from jax import lax
from jax.experimental import pallas as pl
from jax.experimental.pallas import tpu as pltpu
from jax.sharding import PartitionSpec as P

MESH = pl.DeviceIdType.MESH
F32 = jnp.float32
BF16 = jnp.bfloat16
NT_DIMS = (((1,), (1,)), ((), ()))
LANES = 128
PIECE = 4


def nt(a, b, precision=None):
    return lax.dot_general(a, b, NT_DIMS, precision=precision, preferred_element_type=F32)


def split_dot(left, right):
    rows = left.shape[0]
    main = left.astype(BF16)
    rest = (left - main.astype(F32)).astype(BF16)
    both = jnp.dot(jnp.concatenate([main, rest], axis=0), right, preferred_element_type=F32)
    return both[:rows] + both[rows:]


def relay_rounds(nx, ny):
    rounds = []
    d = 1
    while d < max(nx, ny):
        near = [(0, d), (0, -d)] if d < ny else []
        near += [(d, 0), (-d, 0)] if d < nx else []
        rounds.append(near)
        d *= 2
    rounds.append([(s * d, 0) for d in range(1, nx) for s in (1, -1)])
    return rounds


def krylov_kernel(dims, send_rows_hbm, tile_cols_hbm, shifts_hbm, start_hbm, tiles_hbm, basis_out, early_out, gram_out, above_out, *scratch):
    nx, ny, steps, tile_rows, slots, ghosts, tile, width, total = dims
    sums = steps - 1
    size = steps * width
    count = nx * ny
    span = gram_out.shape[1]
    per_column = width // PIECE
    parts = per_column * (span // LANES)
    stride = count // parts
    (send_rows, tile_cols, shifts, small_sem, gram, above, tail_sem, tiles, basis, early, first, tile_sem, out_sem, early_sem, halo_send, halo_recv, relay,
     rs_send, rs_recv, ag_send, ag_recv) = scratch[:21]
    ext = scratch[21:21 + steps]
    outbox = scratch[21 + steps:21 + 2 * steps]
    part = scratch[21 + 2 * steps:21 + 2 * steps + sums]
    landed = scratch[21 + 2 * steps + sums:21 + 2 * steps + 2 * sums]
    full = scratch[21 + 2 * steps + 2 * sums:21 + 2 * steps + 3 * sums]
    ix, iy = lax.axis_index("gx"), lax.axis_index("gy")
    me = ix * ny + iy

    def inside(dx, dy):
        x, y = ix + dx, iy + dy
        return (x >= 0) & (x < nx) & (y >= 0) & (y < ny)

    def tell(sem, offsets):
        for dx, dy in offsets:
            @pl.when(inside(dx, dy))
            def _():
                pl.semaphore_signal(sem, inc=1, device_id=(ix + dx, iy + dy), device_id_type=MESH)

    def heard(sem, offsets):
        pl.semaphore_wait(sem, sum(jnp.where(inside(dx, dy), 1, 0) for dx, dy in offsets))

    sides = [(0, 1), (0, -1), (1, 0), (-1, 0)]
    slot_of = {(1, 0): 0, (-1, 0): 1, (0, 1): 2, (0, -1): 3}
    barrier = pltpu.get_barrier_semaphore()
    tell(barrier, sides)

    small = [
        pltpu.make_async_copy(send_rows_hbm, send_rows, small_sem.at[0]),
        pltpu.make_async_copy(tile_cols_hbm, tile_cols, small_sem.at[1]),
        pltpu.make_async_copy(shifts_hbm, shifts, small_sem.at[2]),
    ]
    for t in range(tile_rows):
        small.append(pltpu.make_async_copy(start_hbm.at[:, t * tile:(t + 1) * tile], first.at[t], small_sem.at[3 + t]))
    for copy in small:
        copy.start()

    def tile_copy(t):
        return pltpu.make_async_copy(tiles_hbm.at[t], tiles.at[t], tile_sem.at[t])


    def edges(j):
        for dx, dy in sides:
            low = tile_rows + slot_of[dx, dy] * ghosts

            @pl.when(jnp.logical_not(inside(-dx, -dy)))
            def _():
                ext[j][low:low + ghosts] = jnp.zeros((ghosts, width, tile), BF16)

    for j in range(steps):
        edges(j)
    for copy in small:
        copy.wait()
    for t in range(tile_rows):
        tile_copy(t).start()
    for s in range(ghosts):
        outbox[0][s] = first[send_rows[0, s]]
    heard(barrier, sides)

    far = jnp.where(lax.rem(ix, 2) == 1, 1, -1)
    far_pair = (far, 0, jnp.where(far == 1, 0, 1), jnp.where(far == 1, 1, 0), 0)
    near_pair = (-far, 0, jnp.where(far == 1, 1, 0), jnp.where(far == 1, 0, 1), 1)
    up_pair = (0, 1, 2, 2, 2)
    down_pair = (0, -1, 3, 3, 3)
    pairs = (far_pair, up_pair, down_pair, near_pair)

    def halo(j, s, pair, incoming=False):
        dx, dy, lands, comes, n = pair
        return pltpu.make_async_remote_copy(
            src_ref=outbox[j].at[s],
            dst_ref=ext[j].at[tile_rows + (comes if incoming else lands) * ghosts + s],
            send_sem=halo_send.at[j, s, n], recv_sem=halo_recv.at[j, s, n],
            device_id=(ix + dx, iy + dy), device_id_type=MESH)

    def halo_start(j, s, some):
        for pair in some:
            @pl.when(inside(pair[0], pair[1]))
            def _():
                halo(j, s, pair).start()

    def halo_wait(j):
        for pair in pairs:
            back = 1 if pair[1] == 0 else -1

            @pl.when(inside(pair[0], back * pair[1]))
            def _():
                for s in range(ghosts):
                    halo(j, s, pair, True).wait_recv()

    def halo_drain(j):
        for pair in pairs:
            @pl.when(inside(pair[0], pair[1]))
            def _():
                for s in range(ghosts):
                    halo(j, s, pair).wait_send()

    for s in range(ghosts):
        halo_start(0, s, pairs[:1])
    for s in range(ghosts):
        halo_start(0, s, pairs[1:])

    ext[0][:tile_rows] = first[...]
    rounds = relay_rounds(nx, ny)
    tell(relay.at[0], rounds[0])
    pending = [0]

    def relay_turn():
        r = pending[0]
        if r < len(rounds):
            heard(relay.at[r], rounds[r])
            if r + 1 < len(rounds):
                tell(relay.at[r + 1], rounds[r + 1])
            pending[0] = r + 1

    def turned(t, c):
        tile_copy(t).wait()
        for k in range(slots):
            tiles[t, k] = tiles[t, k].T
        return c

    half = tile_rows // 2
    lax.fori_loop(0, half, turned, 0)
    relay_turn()
    lax.fori_loop(half, tile_rows, turned, 0)
    basis[(steps - 1) * width:, :] = jnp.zeros((width, basis.shape[1]), BF16)
    relay_turn()

    def row_image(j, r):
        acc = jnp.dot(ext[j][tile_cols[r, 0]], tiles[r, 0], preferred_element_type=F32)
        for k in range(1, slots):
            acc = acc + jnp.dot(ext[j][tile_cols[r, k]], tiles[r, k], preferred_element_type=F32)
        return (acc - shifts[j] * ext[j][r].astype(F32)).astype(BF16)

    def own_part():
        return me // stride

    def when_owner(act):
        if stride == 1:
            act()
        else:
            pl.when(lax.rem(me, stride) == 0)(act)

    def wrap(i, n):
        return jnp.where(i >= n, i - n, i)

    def each_other(act):
        for a in range(nx):
            x = wrap(ix + a, nx)

            def turn(b, c):
                act(x, wrap(iy + b, ny), a * ny + b - 1)
                return c
            lax.fori_loop(0 if a else 1, ny, turn, 0, unroll=4)

    def scatter(u):
        def send(x, y, slot):
            owner = x * ny + y

            def go():
                pltpu.make_async_remote_copy(
                    src_ref=part[u].at[owner // stride], dst_ref=landed[u].at[slot],
                    send_sem=rs_send.at[u], recv_sem=rs_recv.at[u],
                    device_id=(x, y), device_id_type=MESH).start()
            if stride == 1:
                go()
            else:
                pl.when(lax.rem(owner, stride) == 0)(go)
        each_other(send)

    def announce(u):
        p = own_part()

        def send(x, y, slot):
            pltpu.make_async_remote_copy(
                src_ref=full[u].at[p], dst_ref=full[u].at[p],
                send_sem=ag_send.at[u], recv_sem=ag_recv.at[u],
                device_id=(x, y), device_id_type=MESH).start()
        each_other(send)

    def arrived(ref, sem):
        pltpu.make_async_copy(ref, ref, sem).wait()

    def gather(u):
        def act():
            arrived(landed[u], rs_recv.at[u])
            full[u][own_part()] = (jnp.sum(landed[u][...], axis=0) + part[u][own_part()]) / total
            announce(u)
        when_owner(act)

    def but_own(act_all, act_rest):
        if stride == 1:
            act_rest()
        else:
            own = lax.rem(me, stride) == 0
            pl.when(own)(act_rest)
            pl.when(jnp.logical_not(own))(act_all)

    def collect(u):
        but_own(lambda: arrived(full[u], ag_recv.at[u]),
                lambda: arrived(full[u].at[:parts - 1], ag_recv.at[u]))

    def drain_scatter(u):
        but_own(lambda: arrived(part[u], rs_send.at[u]),
                lambda: arrived(part[u].at[:parts - 1], rs_send.at[u]))

    def drain_gather(u):
        when_owner(lambda: arrived(landed[u], ag_send.at[u]))

    def column(u, c):
        low = c * per_column
        return jnp.concatenate([full[u][p] for p in range(low, low + per_column)], axis=0)

    def load_part(u, blocks):
        for c, block in enumerate(blocks):
            for a in range(per_column):
                part[u][c * per_column + a] = block[a * PIECE:(a + 1) * PIECE]

    def basis_copy(j):
        rows = slice(j * width, (j + 1) * width)
        return pltpu.make_async_copy(basis.at[rows], basis_out.at[rows], out_sem.at[j])

    for j in range(steps):
        halo_wait(j)
        if j + 1 < steps:
            for s in range(ghosts):
                outbox[j + 1][s] = row_image(j, send_rows[0, s])
                halo_start(j + 1, s, pairs[:3])
            for s in range(ghosts):
                halo_start(j + 1, s, pairs[3:])

        def row(t, c):
            value = row_image(j, t)
            if j + 1 < steps:
                ext[j + 1][t] = value
            cols = pl.ds(pl.multiple_of(t * tile, tile), tile)
            basis[j * width:(j + 1) * width, cols] = value
            if j + 1 == steps:
                c = c + nt(value, basis[:, cols])
            return c

        carry = jnp.zeros((width, size), F32) if j + 1 == steps else 0
        carry = lax.fori_loop(0, tile_rows, row, carry, unroll=8)
        basis_copy(j).start()
        if j == 0:
            relay_turn()
        elif j == 1:
            local = nt(basis[:2 * width, :], basis[:2 * width, :])
            load_part(0, [local[:width], local[width:]])
            for _ in rounds:
                relay_turn()
            scatter(0)
        else:
            local = carry if j + 1 == steps else nt(basis[j * width:(j + 1) * width, :], basis[...])
            load_part(j - 1, [local[:, c * LANES:(c + 1) * LANES] for c in range(span // LANES)])
            scatter(j - 1)
            gather(j - 2)
    above[...] = jnp.zeros(above.shape, F32)
    collect(0)
    extend_inverse(0, width, column(0, 0)[:, :width], above)
    extend_inverse(1, width, column(0, 1), above)
    gather(steps - 2)
    for u in range(1, steps - 2):
        collect(u)
        wide = jnp.concatenate([column(u, c) for c in range(span // LANES)], axis=1)
        extend_inverse(u + 1, width, wide[:, :(u + 2) * width], above)
    above_copy = pltpu.make_async_copy(above, above_out, tail_sem.at[0])
    above_copy.start()
    done = (steps - 1) * width
    chunk = 2 * tile
    for n in range(basis.shape[1] // chunk):
        cols = slice(n * chunk, (n + 1) * chunk)
        early[:, cols] = split_dot(above[:done, :], basis[:, cols])
    early_copy = pltpu.make_async_copy(early, early_out, early_sem)
    early_copy.start()
    for j in range(steps):
        basis_copy(j).wait()
        halo_drain(j)
    for u in range(sums):
        drain_scatter(u)
        if u + 1 < sums:
            drain_gather(u)
    above_copy.wait()
    collect(sums - 1)
    for c in range(span // LANES):
        gram[:, c * LANES:(c + 1) * LANES] = column(sums - 1, c)
    gram_copy = pltpu.make_async_copy(gram, gram_out, tail_sem.at[1])
    gram_copy.start()
    drain_gather(sums - 1)
    early_copy.wait()
    gram_copy.wait()


def factor(block, midway=None):
    width = block.shape[0]
    count = width // 8
    eye_r = lax.broadcasted_iota(jnp.int32, (width, width), 0)
    eye_c = lax.broadcasted_iota(jnp.int32, (width, width), 1)
    work = jnp.concatenate([block, jnp.where(eye_r == eye_c, 1.0, 0.0).astype(F32)], axis=1)
    rows = lax.broadcasted_iota(jnp.int32, (8, 2 * width), 0)
    groups = [work[g * 8:(g + 1) * 8] for g in range(count)]
    done = []
    for g in range(count):
        if midway is not None and g == count // 2:
            midway()
        cols = [
            [jnp.broadcast_to(groups[h][:, g * 8 + r:g * 8 + r + 1], (8, 2 * width)) for h in range(g, count)]
            for r in range(8)
        ]
        pivots = cols[0][0]
        for r in range(8):
            inverse = 1.0 / cols[r][0][r:r + 1]
            if r:
                pivots = jnp.where(rows == r, cols[r][0], pivots)
            for m in range(r + 1, 8):
                share = cols[m][0][r:r + 1] * inverse
                cols[m] = [c - d * share for c, d in zip(cols[m], cols[r])]
            scaled = groups[g][r:r + 1] * inverse
            for h in range(g, count):
                update = groups[h] - cols[r][h - g] * scaled
                groups[h] = jnp.where(rows > r, update, groups[h]) if h == g else update
        done.append(groups[g] * lax.rsqrt(pivots))
    return jnp.concatenate(done, axis=0)[:, width:]


def extend_inverse(j, width, gram_row, inverse, midway=None):
    high = lax.Precision.HIGHEST
    lo, hi = j * width, (j + 1) * width
    block = gram_row[:, lo:hi]
    if j:
        previous = inverse[0:lo, 0:lo]
        left = nt(gram_row[:, 0:lo], previous, high)
        block = block - nt(left, left, high)
    own = factor(block, midway)
    inverse[lo:hi, lo:hi] = own
    if j:
        cross = jnp.dot(left, previous, precision=high, preferred_element_type=F32)
        inverse[lo:hi, 0:lo] = -jnp.dot(own, cross, precision=high, preferred_element_type=F32)


def finish_kernel(dims, basis_hbm, early_hbm, gram_hbm, above_hbm, out, gram, inverse, basis, early, staged, sem):
    steps, width, chunk = dims
    done = (steps - 1) * width
    gram_in = pltpu.make_async_copy(gram_hbm, gram, sem.at[3])
    above_in = pltpu.make_async_copy(above_hbm, inverse.at[:done], sem.at[4])
    early_in = pltpu.make_async_copy(early_hbm, early, sem.at[0])
    basis_copy = pltpu.make_async_copy(basis_hbm, basis, sem.at[1])
    for copy in (gram_in, above_in, early_in, basis_copy):
        copy.start()
    early_copy = pltpu.make_async_copy(early, out.at[:done], sem.at[2])

    def pass_on():
        early_in.wait()
        early_copy.start()

    gram_in.wait()
    above_in.wait()
    extend_inverse(steps - 1, width, gram[...], inverse, pass_on)
    basis_copy.wait()
    copies = []
    for n in range(basis.shape[1] // chunk):
        cols = slice(n * chunk, (n + 1) * chunk)
        staged[:, cols] = split_dot(inverse[done:, :], basis[:, cols])
        copy = pltpu.make_async_copy(staged.at[:, cols], out.at[done:, cols], sem.at[5 + n])
        copy.start()
        copies.append(copy)
    early_copy.wait()
    for copy in copies:
        copy.wait()


def body(nx, ny, start_block, tiles, tile_cols, send_rows, shifts):
    width, nodes = start_block.shape
    tile_rows, slots, tile, _ = tiles.shape
    ghosts = send_rows.shape[1]
    steps = shifts.shape[0]
    size = steps * width
    done = size - width
    sums = steps - 1
    span = -(-size // LANES) * LANES
    parts = (width // PIECE) * (span // LANES)
    count = nx * ny
    dims = (nx, ny, steps, tile_rows, slots, ghosts, tile, width, nodes * count)
    dma = pltpu.SemaphoreType.DMA
    hbm = pl.BlockSpec(memory_space=pl.ANY)
    basis, early, gram, above = pl.pallas_call(
        functools.partial(krylov_kernel, dims),
        out_shape=(
            jax.ShapeDtypeStruct((size, nodes), BF16),
            jax.ShapeDtypeStruct((done, nodes), F32),
            jax.ShapeDtypeStruct((width, span), F32),
            jax.ShapeDtypeStruct((done, size), F32),
        ),
        in_specs=[hbm] * 5,
        out_specs=(hbm, hbm, hbm, hbm),
        scratch_shapes=[
            pltpu.SMEM(send_rows.shape, jnp.int32),
            pltpu.SMEM(tile_cols.shape, jnp.int32),
            pltpu.SMEM(shifts.shape, F32),
            dma((3 + tile_rows,)),
            pltpu.VMEM((width, span), F32),
            pltpu.VMEM((done, size), F32),
            dma((2,)),
            pltpu.VMEM(tiles.shape, BF16),
            pltpu.VMEM((size, nodes), BF16),
            pltpu.VMEM((done, nodes), F32),
            pltpu.VMEM((tile_rows, width, tile), BF16),
            dma((tile_rows,)), dma((steps,)), dma,
            dma((steps, ghosts, 4)), dma((steps, ghosts, 4)),
            pltpu.SemaphoreType.REGULAR((len(relay_rounds(nx, ny)),)),
            dma((sums,)), dma((sums,)), dma((sums,)), dma((sums,)),
        ]
        + [pltpu.VMEM((tile_rows + 4 * ghosts, width, tile), BF16) for _ in range(steps)]
        + [pltpu.VMEM((ghosts, width, tile), BF16) for _ in range(steps)]
        + [pltpu.VMEM((parts, PIECE, LANES), F32) for _ in range(sums)]
        + [pltpu.VMEM((count - 1, PIECE, LANES), F32) for _ in range(sums)]
        + [pltpu.VMEM((parts, PIECE, LANES), F32) for _ in range(sums)],
        compiler_params=pltpu.CompilerParams(collective_id=0, has_side_effects=True, vmem_limit_bytes=56 * 2**20),
    )(send_rows, tile_cols, shifts, start_block, tiles)
    chunk = 2 * tile
    return pl.pallas_call(
        functools.partial(finish_kernel, (steps, width, chunk)),
        out_shape=jax.ShapeDtypeStruct((size, nodes), F32),
        in_specs=[hbm, hbm, hbm, hbm],
        out_specs=hbm,
        scratch_shapes=[
            pltpu.VMEM((width, span), F32),
            pltpu.VMEM((size, size), F32),
            pltpu.VMEM((size, nodes), BF16),
            pltpu.VMEM((done, nodes), F32),
            pltpu.VMEM((width, nodes), F32),
            dma((5 + nodes // chunk,)),
        ],
        compiler_params=pltpu.CompilerParams(vmem_limit_bytes=56 * 2**20),
    )(basis, early, gram, above)


def solution(mesh):
    in_specs = (
        P(None, ("gx", "gy")),
        P(("gx", "gy"), None, None, None),
        P(("gx", "gy"), None),
        P(("gx", "gy"), None),
        P(),
    )
    out_specs = P(None, ("gx", "gy"))
    run = functools.partial(body, mesh.shape["gx"], mesh.shape["gy"])
    return jax.shard_map(run, mesh=mesh, in_specs=in_specs, out_specs=out_specs, check_vma=False)
```

```python
import functools

import jax
import jax.numpy as jnp
from jax import lax
from jax.experimental import pallas as pl
from jax.experimental.pallas import tpu as pltpu
from jax.sharding import PartitionSpec as P

MESH = pl.DeviceIdType.MESH
F32 = jnp.float32
BF16 = jnp.bfloat16
NT_DIMS = (((1,), (1,)), ((), ()))
LANES = 128
PIECE = 4


def nt(a, b, precision=None):
    return lax.dot_general(a, b, NT_DIMS, precision=precision, preferred_element_type=F32)


def split_dot(left, right):
    rows = left.shape[0]
    main = left.astype(BF16)
    rest = (left - main.astype(F32)).astype(BF16)
    both = jnp.dot(jnp.concatenate([main, rest], axis=0), right, preferred_element_type=F32)
    return both[:rows] + both[rows:]


def relay_rounds(nx, ny):
    rounds = []
    d = 1
    while d < max(nx, ny):
        near = [(0, d), (0, -d)] if d < ny else []
        near += [(d, 0), (-d, 0)] if d < nx else []
        rounds.append(near)
        d *= 2
    rounds.append([(s * d, 0) for d in range(1, nx) for s in (1, -1)])
    return rounds


def krylov_kernel(dims, send_rows_hbm, tile_cols_hbm, shifts_hbm, start_hbm, tiles_hbm, basis_out, early_out, gram_out, above_out, *scratch):
    nx, ny, steps, tile_rows, slots, ghosts, tile, width, total = dims
    sums = steps - 1
    size = steps * width
    count = nx * ny
    span = gram_out.shape[1]
    per_column = width // PIECE
    parts = per_column * (span // LANES)
    stride = count // parts
    (send_rows, tile_cols, shifts, small_sem, gram, above, tail_sem, tiles, basis, early, first, tile_sem, out_sem, early_sem, halo_send, halo_recv, relay,
     rs_send, rs_recv, ag_send, ag_recv) = scratch[:21]
    ext = scratch[21:21 + steps]
    outbox = scratch[21 + steps:21 + 2 * steps]
    part = scratch[21 + 2 * steps:21 + 2 * steps + sums]
    landed = scratch[21 + 2 * steps + sums:21 + 2 * steps + 2 * sums]
    full = scratch[21 + 2 * steps + 2 * sums:21 + 2 * steps + 3 * sums]
    ix, iy = lax.axis_index("gx"), lax.axis_index("gy")
    me = ix * ny + iy

    def inside(dx, dy):
        x, y = ix + dx, iy + dy
        return (x >= 0) & (x < nx) & (y >= 0) & (y < ny)

    def tell(sem, offsets):
        for dx, dy in offsets:
            @pl.when(inside(dx, dy))
            def _():
                pl.semaphore_signal(sem, inc=1, device_id=(ix + dx, iy + dy), device_id_type=MESH)

    def heard(sem, offsets):
        pl.semaphore_wait(sem, sum(jnp.where(inside(dx, dy), 1, 0) for dx, dy in offsets))

    sides = [(0, 1), (0, -1), (1, 0), (-1, 0)]
    slot_of = {(1, 0): 0, (-1, 0): 1, (0, 1): 2, (0, -1): 3}
    barrier = pltpu.get_barrier_semaphore()
    tell(barrier, sides)

    small = [
        pltpu.make_async_copy(send_rows_hbm, send_rows, small_sem.at[0]),
        pltpu.make_async_copy(tile_cols_hbm, tile_cols, small_sem.at[1]),
        pltpu.make_async_copy(shifts_hbm, shifts, small_sem.at[2]),
    ]
    for t in range(tile_rows):
        small.append(pltpu.make_async_copy(start_hbm.at[:, t * tile:(t + 1) * tile], first.at[t], small_sem.at[3 + t]))
    for copy in small:
        copy.start()

    def tile_copy(t):
        return pltpu.make_async_copy(tiles_hbm.at[t], tiles.at[t], tile_sem.at[t])


    def edges(j):
        for dx, dy in sides:
            low = tile_rows + slot_of[dx, dy] * ghosts

            @pl.when(jnp.logical_not(inside(-dx, -dy)))
            def _():
                ext[j][low:low + ghosts] = jnp.zeros((ghosts, width, tile), BF16)

    for j in range(steps):
        edges(j)
    for copy in small:
        copy.wait()
    for t in range(tile_rows):
        tile_copy(t).start()
    for s in range(ghosts):
        outbox[0][s] = first[send_rows[0, s]]
    heard(barrier, sides)

    far = jnp.where(lax.rem(ix, 2) == 1, 1, -1)
    far_pair = (far, 0, jnp.where(far == 1, 0, 1), jnp.where(far == 1, 1, 0), 0)
    near_pair = (-far, 0, jnp.where(far == 1, 1, 0), jnp.where(far == 1, 0, 1), 1)
    up_pair = (0, 1, 2, 2, 2)
    down_pair = (0, -1, 3, 3, 3)
    pairs = (far_pair, up_pair, down_pair, near_pair)

    def halo(j, s, pair, incoming=False):
        dx, dy, lands, comes, n = pair
        return pltpu.make_async_remote_copy(
            src_ref=outbox[j].at[s],
            dst_ref=ext[j].at[tile_rows + (comes if incoming else lands) * ghosts + s],
            send_sem=halo_send.at[j, s, n], recv_sem=halo_recv.at[j, s, n],
            device_id=(ix + dx, iy + dy), device_id_type=MESH)

    def halo_start(j, s, some):
        for pair in some:
            @pl.when(inside(pair[0], pair[1]))
            def _():
                halo(j, s, pair).start()

    def halo_wait(j):
        for pair in pairs:
            back = 1 if pair[1] == 0 else -1

            @pl.when(inside(pair[0], back * pair[1]))
            def _():
                for s in range(ghosts):
                    halo(j, s, pair, True).wait_recv()

    def halo_drain(j):
        for pair in pairs:
            @pl.when(inside(pair[0], pair[1]))
            def _():
                for s in range(ghosts):
                    halo(j, s, pair).wait_send()

    for s in range(ghosts):
        halo_start(0, s, pairs[:1])
    for s in range(ghosts):
        halo_start(0, s, pairs[1:])

    ext[0][:tile_rows] = first[...]
    rounds = relay_rounds(nx, ny)
    tell(relay.at[0], rounds[0])
    pending = [0]

    def relay_turn():
        r = pending[0]
        if r < len(rounds):
            heard(relay.at[r], rounds[r])
            if r + 1 < len(rounds):
                tell(relay.at[r + 1], rounds[r + 1])
            pending[0] = r + 1

    def turned(t, c):
        tile_copy(t).wait()
        for k in range(slots):
            tiles[t, k] = tiles[t, k].T
        return c

    half = tile_rows // 2
    lax.fori_loop(0, half, turned, 0)
    relay_turn()
    lax.fori_loop(half, tile_rows, turned, 0)
    basis[(steps - 1) * width:, :] = jnp.zeros((width, basis.shape[1]), BF16)
    relay_turn()

    def row_image(j, r):
        acc = jnp.dot(ext[j][tile_cols[r, 0]], tiles[r, 0], preferred_element_type=F32)
        for k in range(1, slots):
            acc = acc + jnp.dot(ext[j][tile_cols[r, k]], tiles[r, k], preferred_element_type=F32)
        return (acc - shifts[j] * ext[j][r].astype(F32)).astype(BF16)

    def own_part():
        return me // stride

    def when_owner(act):
        if stride == 1:
            act()
        else:
            pl.when(lax.rem(me, stride) == 0)(act)

    def wrap(i, n):
        return jnp.where(i >= n, i - n, i)

    def each_other(act):
        for a in reversed(range(nx)):
            x = wrap(ix + a, nx)

            def turn(b, c):
                act(x, wrap(iy + b, ny), a * ny + b - 1)
                return c
            lax.fori_loop(0 if a else 1, ny, turn, 0, unroll=8 if ny <= 8 else 4)

    def scatter(u):
        def send(x, y, slot):
            owner = x * ny + y

            def go():
                pltpu.make_async_remote_copy(
                    src_ref=part[u].at[owner // stride], dst_ref=landed[u].at[slot],
                    send_sem=rs_send.at[u], recv_sem=rs_recv.at[u],
                    device_id=(x, y), device_id_type=MESH).start()
            if stride == 1:
                go()
            else:
                pl.when(lax.rem(owner, stride) == 0)(go)
        each_other(send)

    def announce(u):
        p = own_part()

        def send(x, y, slot):
            pltpu.make_async_remote_copy(
                src_ref=full[u].at[p], dst_ref=full[u].at[p],
                send_sem=ag_send.at[u], recv_sem=ag_recv.at[u],
                device_id=(x, y), device_id_type=MESH).start()
        each_other(send)

    def arrived(ref, sem):
        pltpu.make_async_copy(ref, ref, sem).wait()

    def gather(u):
        def act():
            arrived(landed[u], rs_recv.at[u])
            full[u][own_part()] = (jnp.sum(landed[u][...], axis=0) + part[u][own_part()]) / total
            announce(u)
        when_owner(act)

    def but_own(act_all, act_rest):
        if stride == 1:
            act_rest()
        else:
            own = lax.rem(me, stride) == 0
            pl.when(own)(act_rest)
            pl.when(jnp.logical_not(own))(act_all)

    def collect(u):
        but_own(lambda: arrived(full[u], ag_recv.at[u]),
                lambda: arrived(full[u].at[:parts - 1], ag_recv.at[u]))

    def drain_scatter(u):
        but_own(lambda: arrived(part[u], rs_send.at[u]),
                lambda: arrived(part[u].at[:parts - 1], rs_send.at[u]))

    def drain_gather(u):
        when_owner(lambda: arrived(landed[u], ag_send.at[u]))

    def column(u, c):
        low = c * per_column
        return jnp.concatenate([full[u][p] for p in range(low, low + per_column)], axis=0)

    def load_part(u, blocks):
        for c, block in enumerate(blocks):
            for a in range(per_column):
                part[u][c * per_column + a] = block[a * PIECE:(a + 1) * PIECE]

    def basis_copy(j):
        rows = slice(j * width, (j + 1) * width)
        return pltpu.make_async_copy(basis.at[rows], basis_out.at[rows], out_sem.at[j])

    for j in range(steps):
        halo_wait(j)
        if j + 1 < steps:
            for s in range(ghosts):
                outbox[j + 1][s] = row_image(j, send_rows[0, s])
                halo_start(j + 1, s, pairs[:3])
            for s in range(ghosts):
                halo_start(j + 1, s, pairs[3:])

        def row(t, c):
            value = row_image(j, t)
            if j + 1 < steps:
                ext[j + 1][t] = value
            cols = pl.ds(pl.multiple_of(t * tile, tile), tile)
            basis[j * width:(j + 1) * width, cols] = value
            if j + 1 == steps:
                c = c + nt(value, basis[:, cols])
            return c

        carry = jnp.zeros((width, size), F32) if j + 1 == steps else 0
        carry = lax.fori_loop(0, tile_rows, row, carry, unroll=8)
        basis_copy(j).start()
        if j == 0:
            relay_turn()
        elif j == 1:
            local = nt(basis[:2 * width, :], basis[:2 * width, :])
            load_part(0, [local[:width], local[width:]])
            for _ in rounds:
                relay_turn()
            scatter(0)
        else:
            local = carry if j + 1 == steps else nt(basis[j * width:(j + 1) * width, :], basis[...])
            load_part(j - 1, [local[:, c * LANES:(c + 1) * LANES] for c in range(span // LANES)])
            scatter(j - 1)
            gather(j - 2)
    above[...] = jnp.zeros(above.shape, F32)
    collect(0)
    extend_inverse(0, width, column(0, 0)[:, :width], above)
    extend_inverse(1, width, column(0, 1), above)
    gather(steps - 2)
    for u in range(1, steps - 2):
        collect(u)
        wide = jnp.concatenate([column(u, c) for c in range(span // LANES)], axis=1)
        extend_inverse(u + 1, width, wide[:, :(u + 2) * width], above)
    above_copy = pltpu.make_async_copy(above, above_out, tail_sem.at[0])
    above_copy.start()
    done = (steps - 1) * width
    chunk = 2 * tile
    for n in range(basis.shape[1] // chunk):
        cols = slice(n * chunk, (n + 1) * chunk)
        early[:, cols] = split_dot(above[:done, :], basis[:, cols])
    early_copy = pltpu.make_async_copy(early, early_out, early_sem)
    early_copy.start()
    for j in range(steps):
        basis_copy(j).wait()
        halo_drain(j)
    for u in range(sums):
        drain_scatter(u)
        if u + 1 < sums:
            drain_gather(u)
    above_copy.wait()
    collect(sums - 1)
    for c in range(span // LANES):
        gram[:, c * LANES:(c + 1) * LANES] = column(sums - 1, c)
    gram_copy = pltpu.make_async_copy(gram, gram_out, tail_sem.at[1])
    gram_copy.start()
    drain_gather(sums - 1)
    early_copy.wait()
    gram_copy.wait()


def factor(block, midway=None):
    width = block.shape[0]
    count = width // 8
    eye_r = lax.broadcasted_iota(jnp.int32, (width, width), 0)
    eye_c = lax.broadcasted_iota(jnp.int32, (width, width), 1)
    work = jnp.concatenate([block, jnp.where(eye_r == eye_c, 1.0, 0.0).astype(F32)], axis=1)
    rows = lax.broadcasted_iota(jnp.int32, (8, 2 * width), 0)
    groups = [work[g * 8:(g + 1) * 8] for g in range(count)]
    done = []
    for g in range(count):
        if midway is not None and g == count // 2:
            midway()
        cols = [
            [jnp.broadcast_to(groups[h][:, g * 8 + r:g * 8 + r + 1], (8, 2 * width)) for h in range(g, count)]
            for r in range(8)
        ]
        pivots = cols[0][0]
        for r in range(8):
            inverse = 1.0 / cols[r][0][r:r + 1]
            if r:
                pivots = jnp.where(rows == r, cols[r][0], pivots)
            for m in range(r + 1, 8):
                share = cols[m][0][r:r + 1] * inverse
                cols[m] = [c - d * share for c, d in zip(cols[m], cols[r])]
            scaled = groups[g][r:r + 1] * inverse
            for h in range(g, count):
                update = groups[h] - cols[r][h - g] * scaled
                groups[h] = jnp.where(rows > r, update, groups[h]) if h == g else update
        done.append(groups[g] * lax.rsqrt(pivots))
    return jnp.concatenate(done, axis=0)[:, width:]


def extend_inverse(j, width, gram_row, inverse, midway=None):
    high = lax.Precision.HIGHEST
    lo, hi = j * width, (j + 1) * width
    block = gram_row[:, lo:hi]
    if j:
        previous = inverse[0:lo, 0:lo]
        left = nt(gram_row[:, 0:lo], previous, high)
        block = block - nt(left, left, high)
    own = factor(block, midway)
    inverse[lo:hi, lo:hi] = own
    if j:
        cross = jnp.dot(left, previous, precision=high, preferred_element_type=F32)
        inverse[lo:hi, 0:lo] = -jnp.dot(own, cross, precision=high, preferred_element_type=F32)


def finish_kernel(dims, basis_hbm, early_hbm, gram_hbm, above_hbm, out, gram, inverse, basis, early, staged, sem):
    steps, width, chunk = dims
    done = (steps - 1) * width
    gram_in = pltpu.make_async_copy(gram_hbm, gram, sem.at[3])
    above_in = pltpu.make_async_copy(above_hbm, inverse.at[:done], sem.at[4])
    early_in = pltpu.make_async_copy(early_hbm, early, sem.at[0])
    basis_copy = pltpu.make_async_copy(basis_hbm, basis, sem.at[1])
    for copy in (gram_in, above_in, early_in, basis_copy):
        copy.start()
    early_copy = pltpu.make_async_copy(early, out.at[:done], sem.at[2])

    def pass_on():
        early_in.wait()
        early_copy.start()

    gram_in.wait()
    above_in.wait()
    extend_inverse(steps - 1, width, gram[...], inverse, pass_on)
    basis_copy.wait()
    copies = []
    for n in range(basis.shape[1] // chunk):
        cols = slice(n * chunk, (n + 1) * chunk)
        staged[:, cols] = split_dot(inverse[done:, :], basis[:, cols])
        copy = pltpu.make_async_copy(staged.at[:, cols], out.at[done:, cols], sem.at[5 + n])
        copy.start()
        copies.append(copy)
    early_copy.wait()
    for copy in copies:
        copy.wait()


def body(nx, ny, start_block, tiles, tile_cols, send_rows, shifts):
    width, nodes = start_block.shape
    tile_rows, slots, tile, _ = tiles.shape
    ghosts = send_rows.shape[1]
    steps = shifts.shape[0]
    size = steps * width
    done = size - width
    sums = steps - 1
    span = -(-size // LANES) * LANES
    parts = (width // PIECE) * (span // LANES)
    count = nx * ny
    dims = (nx, ny, steps, tile_rows, slots, ghosts, tile, width, nodes * count)
    dma = pltpu.SemaphoreType.DMA
    hbm = pl.BlockSpec(memory_space=pl.ANY)
    basis, early, gram, above = pl.pallas_call(
        functools.partial(krylov_kernel, dims),
        out_shape=(
            jax.ShapeDtypeStruct((size, nodes), BF16),
            jax.ShapeDtypeStruct((done, nodes), F32),
            jax.ShapeDtypeStruct((width, span), F32),
            jax.ShapeDtypeStruct((done, size), F32),
        ),
        in_specs=[hbm] * 5,
        out_specs=(hbm, hbm, hbm, hbm),
        scratch_shapes=[
            pltpu.SMEM(send_rows.shape, jnp.int32),
            pltpu.SMEM(tile_cols.shape, jnp.int32),
            pltpu.SMEM(shifts.shape, F32),
            dma((3 + tile_rows,)),
            pltpu.VMEM((width, span), F32),
            pltpu.VMEM((done, size), F32),
            dma((2,)),
            pltpu.VMEM(tiles.shape, BF16),
            pltpu.VMEM((size, nodes), BF16),
            pltpu.VMEM((done, nodes), F32),
            pltpu.VMEM((tile_rows, width, tile), BF16),
            dma((tile_rows,)), dma((steps,)), dma,
            dma((steps, ghosts, 4)), dma((steps, ghosts, 4)),
            pltpu.SemaphoreType.REGULAR((len(relay_rounds(nx, ny)),)),
            dma((sums,)), dma((sums,)), dma((sums,)), dma((sums,)),
        ]
        + [pltpu.VMEM((tile_rows + 4 * ghosts, width, tile), BF16) for _ in range(steps)]
        + [pltpu.VMEM((ghosts, width, tile), BF16) for _ in range(steps)]
        + [pltpu.VMEM((parts, PIECE, LANES), F32) for _ in range(sums)]
        + [pltpu.VMEM((count - 1, PIECE, LANES), F32) for _ in range(sums)]
        + [pltpu.VMEM((parts, PIECE, LANES), F32) for _ in range(sums)],
        compiler_params=pltpu.CompilerParams(collective_id=0, has_side_effects=True, vmem_limit_bytes=56 * 2**20),
    )(send_rows, tile_cols, shifts, start_block, tiles)
    chunk = 2 * tile
    return pl.pallas_call(
        functools.partial(finish_kernel, (steps, width, chunk)),
        out_shape=jax.ShapeDtypeStruct((size, nodes), F32),
        in_specs=[hbm, hbm, hbm, hbm],
        out_specs=hbm,
        scratch_shapes=[
            pltpu.VMEM((width, span), F32),
            pltpu.VMEM((size, size), F32),
            pltpu.VMEM((size, nodes), BF16),
            pltpu.VMEM((done, nodes), F32),
            pltpu.VMEM((width, nodes), F32),
            dma((5 + nodes // chunk,)),
        ],
        compiler_params=pltpu.CompilerParams(vmem_limit_bytes=56 * 2**20),
    )(basis, early, gram, above)


def solution(mesh):
    in_specs = (
        P(None, ("gx", "gy")),
        P(("gx", "gy"), None, None, None),
        P(("gx", "gy"), None),
        P(("gx", "gy"), None),
        P(),
    )
    out_specs = P(None, ("gx", "gy"))
    run = functools.partial(body, mesh.shape["gx"], mesh.shape["gy"])
    return jax.shard_map(run, mesh=mesh, in_specs=in_specs, out_specs=out_specs, check_vma=False)
```

```python
import functools

import jax
import jax.numpy as jnp
from jax import lax
from jax.experimental import pallas as pl
from jax.experimental.pallas import tpu as pltpu
from jax.sharding import PartitionSpec as P

MESH = pl.DeviceIdType.MESH
F32 = jnp.float32
BF16 = jnp.bfloat16
NT_DIMS = (((1,), (1,)), ((), ()))
LANES = 128
PIECE = 4


def nt(a, b, precision=None):
    return lax.dot_general(a, b, NT_DIMS, precision=precision, preferred_element_type=F32)


def split_dot(left, right):
    rows = left.shape[0]
    main = left.astype(BF16)
    rest = (left - main.astype(F32)).astype(BF16)
    both = jnp.dot(jnp.concatenate([main, rest], axis=0), right, preferred_element_type=F32)
    return both[:rows] + both[rows:]


def relay_rounds(nx, ny):
    rounds = []
    d = 1
    while d < max(nx, ny):
        near = [(0, d), (0, -d)] if d < ny else []
        near += [(d, 0), (-d, 0)] if d < nx else []
        rounds.append(near)
        d *= 2
    rounds.append([(s * d, 0) for d in range(1, nx) for s in (1, -1)])
    return rounds


def krylov_kernel(dims, send_rows_hbm, tile_cols_hbm, shifts_hbm, start_hbm, tiles_hbm, basis_out, early_out, gram_out, above_out, *scratch):
    nx, ny, steps, tile_rows, slots, ghosts, tile, width, total = dims
    sums = steps - 1
    size = steps * width
    count = nx * ny
    span = gram_out.shape[1]
    per_column = width // PIECE
    parts = per_column * (span // LANES)
    stride = count // parts
    (send_rows, tile_cols, shifts, small_sem, gram, above, tail_sem, tiles, basis, early, first, tile_sem, out_sem, early_sem, halo_send, halo_recv, relay,
     rs_send, rs_recv, ag_send, ag_recv) = scratch[:21]
    ext = scratch[21:21 + steps]
    outbox = scratch[21 + steps:21 + 2 * steps]
    part = scratch[21 + 2 * steps:21 + 2 * steps + sums]
    landed = scratch[21 + 2 * steps + sums:21 + 2 * steps + 2 * sums]
    full = scratch[21 + 2 * steps + 2 * sums:21 + 2 * steps + 3 * sums]
    ix, iy = lax.axis_index("gx"), lax.axis_index("gy")
    me = ix * ny + iy

    def inside(dx, dy):
        x, y = ix + dx, iy + dy
        return (x >= 0) & (x < nx) & (y >= 0) & (y < ny)

    def tell(sem, offsets):
        for dx, dy in offsets:
            @pl.when(inside(dx, dy))
            def _():
                pl.semaphore_signal(sem, inc=1, device_id=(ix + dx, iy + dy), device_id_type=MESH)

    def heard(sem, offsets):
        pl.semaphore_wait(sem, sum(jnp.where(inside(dx, dy), 1, 0) for dx, dy in offsets))

    sides = [(0, 1), (0, -1), (1, 0), (-1, 0)]
    slot_of = {(1, 0): 0, (-1, 0): 1, (0, 1): 2, (0, -1): 3}
    barrier = pltpu.get_barrier_semaphore()
    tell(barrier, sides)

    small = [
        pltpu.make_async_copy(send_rows_hbm, send_rows, small_sem.at[0]),
        pltpu.make_async_copy(tile_cols_hbm, tile_cols, small_sem.at[1]),
        pltpu.make_async_copy(shifts_hbm, shifts, small_sem.at[2]),
    ]
    for t in range(tile_rows):
        small.append(pltpu.make_async_copy(start_hbm.at[:, t * tile:(t + 1) * tile], first.at[t], small_sem.at[3 + t]))
    for copy in small:
        copy.start()

    def tile_copy(t):
        return pltpu.make_async_copy(tiles_hbm.at[t], tiles.at[t], tile_sem.at[t])


    def edges(j):
        for dx, dy in sides:
            low = tile_rows + slot_of[dx, dy] * ghosts

            @pl.when(jnp.logical_not(inside(-dx, -dy)))
            def _():
                ext[j][low:low + ghosts] = jnp.zeros((ghosts, width, tile), BF16)

    for copy in small:
        copy.wait()
    for t in range(tile_rows):
        tile_copy(t).start()
    for s in range(ghosts):
        outbox[0][s] = first[send_rows[0, s]]
    heard(barrier, sides)

    far = jnp.where(lax.rem(ix, 2) == 1, 1, -1)
    far_pair = (far, 0, jnp.where(far == 1, 0, 1), jnp.where(far == 1, 1, 0), 0)
    near_pair = (-far, 0, jnp.where(far == 1, 1, 0), jnp.where(far == 1, 0, 1), 1)
    up_pair = (0, 1, 2, 2, 2)
    down_pair = (0, -1, 3, 3, 3)
    pairs = (far_pair, up_pair, down_pair, near_pair)

    def halo(j, s, pair, incoming=False):
        dx, dy, lands, comes, n = pair
        if n == 1:
            return pltpu.make_async_remote_copy(
                src_ref=outbox[j],
                dst_ref=ext[j].at[pl.ds(tile_rows + (comes if incoming else lands) * ghosts, ghosts)],
                send_sem=halo_send.at[j, 0, n], recv_sem=halo_recv.at[j, 0, n],
                device_id=(ix + dx, iy + dy), device_id_type=MESH)
        return pltpu.make_async_remote_copy(
            src_ref=outbox[j].at[s],
            dst_ref=ext[j].at[tile_rows + (comes if incoming else lands) * ghosts + s],
            send_sem=halo_send.at[j, s, n], recv_sem=halo_recv.at[j, s, n],
            device_id=(ix + dx, iy + dy), device_id_type=MESH)

    def halo_start(j, s, some):
        for pair in some:
            @pl.when(inside(pair[0], pair[1]))
            def _():
                halo(j, s, pair).start()

    def halo_wait(j):
        for pair in pairs:
            back = 1 if pair[1] == 0 else -1

            @pl.when(inside(pair[0], back * pair[1]))
            def _():
                for s in range(1 if pair is near_pair else ghosts):
                    halo(j, s, pair, True).wait_recv()

    def halo_drain(j):
        for pair in pairs:
            @pl.when(inside(pair[0], pair[1]))
            def _():
                for s in range(1 if pair is near_pair else ghosts):
                    halo(j, s, pair).wait_send()

    for s in range(ghosts):
        halo_start(0, s, pairs[:1])
    for s in range(ghosts):
        halo_start(0, s, pairs[1:3])
    halo_start(0, 0, pairs[3:])

    for j in range(steps):
        edges(j)
    ext[0][:tile_rows] = first[...]
    rounds = relay_rounds(nx, ny)
    tell(relay.at[0], rounds[0])
    pending = [0]

    def relay_turn():
        r = pending[0]
        if r < len(rounds):
            heard(relay.at[r], rounds[r])
            if r + 1 < len(rounds):
                tell(relay.at[r + 1], rounds[r + 1])
            pending[0] = r + 1

    def turned(t, c):
        tile_copy(t).wait()
        for k in range(slots):
            tiles[t, k] = tiles[t, k].T
        return c

    half = tile_rows // 2
    lax.fori_loop(0, half, turned, 0)
    relay_turn()
    lax.fori_loop(half, tile_rows, turned, 0)
    basis[(steps - 1) * width:, :] = jnp.zeros((width, basis.shape[1]), BF16)
    relay_turn()

    def row_image(j, r):
        acc = jnp.dot(ext[j][tile_cols[r, 0]], tiles[r, 0], preferred_element_type=F32)
        for k in range(1, slots):
            acc = acc + jnp.dot(ext[j][tile_cols[r, k]], tiles[r, k], preferred_element_type=F32)
        return (acc - shifts[j] * ext[j][r].astype(F32)).astype(BF16)

    def own_part():
        return me // stride

    def when_owner(act):
        if stride == 1:
            act()
        else:
            pl.when(lax.rem(me, stride) == 0)(act)

    def wrap(i, n):
        return jnp.where(i >= n, i - n, i)

    def each_other(act):
        for a in reversed(range(nx)):
            x = wrap(ix + a, nx)

            def turn(b, c):
                act(x, wrap(iy + b, ny), a * ny + b - 1)
                return c
            lax.fori_loop(0 if a else 1, ny, turn, 0, unroll=8 if ny <= 8 else 4)

    def scatter(u):
        def send(x, y, slot):
            owner = x * ny + y

            def go():
                pltpu.make_async_remote_copy(
                    src_ref=part[u].at[owner // stride], dst_ref=landed[u].at[slot],
                    send_sem=rs_send.at[u], recv_sem=rs_recv.at[u],
                    device_id=(x, y), device_id_type=MESH).start()
            if stride == 1:
                go()
            else:
                pl.when(lax.rem(owner, stride) == 0)(go)
        each_other(send)

    def announce(u):
        p = own_part()

        def send(x, y, slot):
            pltpu.make_async_remote_copy(
                src_ref=full[u].at[p], dst_ref=full[u].at[p],
                send_sem=ag_send.at[u], recv_sem=ag_recv.at[u],
                device_id=(x, y), device_id_type=MESH).start()
        each_other(send)

    def arrived(ref, sem):
        pltpu.make_async_copy(ref, ref, sem).wait()

    def gather(u):
        def act():
            arrived(landed[u], rs_recv.at[u])
            full[u][own_part()] = (jnp.sum(landed[u][...], axis=0) + part[u][own_part()]) / total
            announce(u)
        when_owner(act)

    def but_own(act_all, act_rest):
        if stride == 1:
            act_rest()
        else:
            own = lax.rem(me, stride) == 0
            pl.when(own)(act_rest)
            pl.when(jnp.logical_not(own))(act_all)

    def collect(u):
        but_own(lambda: arrived(full[u], ag_recv.at[u]),
                lambda: arrived(full[u].at[:parts - 1], ag_recv.at[u]))

    def drain_scatter(u):
        but_own(lambda: arrived(part[u], rs_send.at[u]),
                lambda: arrived(part[u].at[:parts - 1], rs_send.at[u]))

    def drain_gather(u):
        when_owner(lambda: arrived(landed[u], ag_send.at[u]))

    def column(u, c):
        low = c * per_column
        return jnp.concatenate([full[u][p] for p in range(low, low + per_column)], axis=0)

    def load_part(u, blocks):
        for c, block in enumerate(blocks):
            for a in range(per_column):
                part[u][c * per_column + a] = block[a * PIECE:(a + 1) * PIECE]

    def basis_copy(j):
        rows = slice(j * width, (j + 1) * width)
        return pltpu.make_async_copy(basis.at[rows], basis_out.at[rows], out_sem.at[j])

    for j in range(steps):
        halo_wait(j)
        if j + 1 < steps:
            for s in range(ghosts):
                outbox[j + 1][s] = row_image(j, send_rows[0, s])
                halo_start(j + 1, s, pairs[:3])
            halo_start(j + 1, 0, pairs[3:])

        def row(t, c):
            value = row_image(j, t)
            if j + 1 < steps:
                ext[j + 1][t] = value
            cols = pl.ds(pl.multiple_of(t * tile, tile), tile)
            basis[j * width:(j + 1) * width, cols] = value
            if j + 1 == steps:
                c = c + nt(value, basis[:, cols])
            return c

        carry = jnp.zeros((width, size), F32) if j + 1 == steps else 0
        carry = lax.fori_loop(0, tile_rows, row, carry, unroll=8)
        basis_copy(j).start()
        if j == 0:
            relay_turn()
        elif j == 1:
            local = nt(basis[:2 * width, :], basis[:2 * width, :])
            load_part(0, [local[:width], local[width:]])
            for _ in rounds:
                relay_turn()
            scatter(0)
        else:
            local = carry if j + 1 == steps else nt(basis[j * width:(j + 1) * width, :], basis[...])
            load_part(j - 1, [local[:, c * LANES:(c + 1) * LANES] for c in range(span // LANES)])
            scatter(j - 1)
            gather(j - 2)
    above[...] = jnp.zeros(above.shape, F32)
    collect(0)
    extend_inverse(0, width, column(0, 0)[:, :width], above)
    extend_inverse(1, width, column(0, 1), above)
    gather(steps - 2)
    for u in range(1, steps - 2):
        collect(u)
        wide = jnp.concatenate([column(u, c) for c in range(span // LANES)], axis=1)
        extend_inverse(u + 1, width, wide[:, :(u + 2) * width], above)
    above_copy = pltpu.make_async_copy(above, above_out, tail_sem.at[0])
    above_copy.start()
    done = (steps - 1) * width
    chunk = 2 * tile
    for n in range(basis.shape[1] // chunk):
        cols = slice(n * chunk, (n + 1) * chunk)
        early[:, cols] = split_dot(above[:done, :], basis[:, cols])
    early_copy = pltpu.make_async_copy(early, early_out, early_sem)
    early_copy.start()
    for j in range(steps):
        basis_copy(j).wait()
        halo_drain(j)
    for u in range(sums):
        drain_scatter(u)
        if u + 1 < sums:
            drain_gather(u)
    above_copy.wait()
    collect(sums - 1)
    for c in range(span // LANES):
        gram[:, c * LANES:(c + 1) * LANES] = column(sums - 1, c)
    gram_copy = pltpu.make_async_copy(gram, gram_out, tail_sem.at[1])
    gram_copy.start()
    drain_gather(sums - 1)
    early_copy.wait()
    gram_copy.wait()


def factor(block, midway=None):
    width = block.shape[0]
    count = width // 8
    eye_r = lax.broadcasted_iota(jnp.int32, (width, width), 0)
    eye_c = lax.broadcasted_iota(jnp.int32, (width, width), 1)
    work = jnp.concatenate([block, jnp.where(eye_r == eye_c, 1.0, 0.0).astype(F32)], axis=1)
    rows = lax.broadcasted_iota(jnp.int32, (8, 2 * width), 0)
    groups = [work[g * 8:(g + 1) * 8] for g in range(count)]
    done = []
    for g in range(count):
        if midway is not None and g == count // 2:
            midway()
        cols = [
            [jnp.broadcast_to(groups[h][:, g * 8 + r:g * 8 + r + 1], (8, 2 * width)) for h in range(g, count)]
            for r in range(8)
        ]
        pivots = cols[0][0]
        for r in range(8):
            inverse = 1.0 / cols[r][0][r:r + 1]
            if r:
                pivots = jnp.where(rows == r, cols[r][0], pivots)
            for m in range(r + 1, 8):
                share = cols[m][0][r:r + 1] * inverse
                cols[m] = [c - d * share for c, d in zip(cols[m], cols[r])]
            scaled = groups[g][r:r + 1] * inverse
            for h in range(g, count):
                update = groups[h] - cols[r][h - g] * scaled
                groups[h] = jnp.where(rows > r, update, groups[h]) if h == g else update
        done.append(groups[g] * lax.rsqrt(pivots))
    return jnp.concatenate(done, axis=0)[:, width:]


def extend_inverse(j, width, gram_row, inverse, midway=None):
    high = lax.Precision.HIGHEST
    lo, hi = j * width, (j + 1) * width
    block = gram_row[:, lo:hi]
    if j:
        previous = inverse[0:lo, 0:lo]
        left = nt(gram_row[:, 0:lo], previous, high)
        block = block - nt(left, left, high)
    own = factor(block, midway)
    inverse[lo:hi, lo:hi] = own
    if j:
        cross = jnp.dot(left, previous, precision=high, preferred_element_type=F32)
        inverse[lo:hi, 0:lo] = -jnp.dot(own, cross, precision=high, preferred_element_type=F32)


def finish_kernel(dims, basis_hbm, early_hbm, gram_hbm, above_hbm, out, gram, inverse, basis, early, staged, sem):
    steps, width, chunk = dims
    done = (steps - 1) * width
    gram_in = pltpu.make_async_copy(gram_hbm, gram, sem.at[3])
    above_in = pltpu.make_async_copy(above_hbm, inverse.at[:done], sem.at[4])
    early_in = pltpu.make_async_copy(early_hbm, early, sem.at[0])
    basis_copy = pltpu.make_async_copy(basis_hbm, basis, sem.at[1])
    for copy in (gram_in, above_in, early_in, basis_copy):
        copy.start()
    early_copy = pltpu.make_async_copy(early, out.at[:done], sem.at[2])

    def pass_on():
        early_in.wait()
        early_copy.start()

    gram_in.wait()
    above_in.wait()
    extend_inverse(steps - 1, width, gram[...], inverse, pass_on)
    basis_copy.wait()
    copies = []
    for n in range(basis.shape[1] // chunk):
        cols = slice(n * chunk, (n + 1) * chunk)
        staged[:, cols] = split_dot(inverse[done:, :], basis[:, cols])
        copy = pltpu.make_async_copy(staged.at[:, cols], out.at[done:, cols], sem.at[5 + n])
        copy.start()
        copies.append(copy)
    early_copy.wait()
    for copy in copies:
        copy.wait()


def body(nx, ny, start_block, tiles, tile_cols, send_rows, shifts):
    width, nodes = start_block.shape
    tile_rows, slots, tile, _ = tiles.shape
    ghosts = send_rows.shape[1]
    steps = shifts.shape[0]
    size = steps * width
    done = size - width
    sums = steps - 1
    span = -(-size // LANES) * LANES
    parts = (width // PIECE) * (span // LANES)
    count = nx * ny
    dims = (nx, ny, steps, tile_rows, slots, ghosts, tile, width, nodes * count)
    dma = pltpu.SemaphoreType.DMA
    hbm = pl.BlockSpec(memory_space=pl.ANY)
    basis, early, gram, above = pl.pallas_call(
        functools.partial(krylov_kernel, dims),
        out_shape=(
            jax.ShapeDtypeStruct((size, nodes), BF16),
            jax.ShapeDtypeStruct((done, nodes), F32),
            jax.ShapeDtypeStruct((width, span), F32),
            jax.ShapeDtypeStruct((done, size), F32),
        ),
        in_specs=[hbm] * 5,
        out_specs=(hbm, hbm, hbm, hbm),
        scratch_shapes=[
            pltpu.SMEM(send_rows.shape, jnp.int32),
            pltpu.SMEM(tile_cols.shape, jnp.int32),
            pltpu.SMEM(shifts.shape, F32),
            dma((3 + tile_rows,)),
            pltpu.VMEM((width, span), F32),
            pltpu.VMEM((done, size), F32),
            dma((2,)),
            pltpu.VMEM(tiles.shape, BF16),
            pltpu.VMEM((size, nodes), BF16),
            pltpu.VMEM((done, nodes), F32),
            pltpu.VMEM((tile_rows, width, tile), BF16),
            dma((tile_rows,)), dma((steps,)), dma,
            dma((steps, ghosts, 4)), dma((steps, ghosts, 4)),
            pltpu.SemaphoreType.REGULAR((len(relay_rounds(nx, ny)),)),
            dma((sums,)), dma((sums,)), dma((sums,)), dma((sums,)),
        ]
        + [pltpu.VMEM((tile_rows + 4 * ghosts, width, tile), BF16) for _ in range(steps)]
        + [pltpu.VMEM((ghosts, width, tile), BF16) for _ in range(steps)]
        + [pltpu.VMEM((parts, PIECE, LANES), F32) for _ in range(sums)]
        + [pltpu.VMEM((count - 1, PIECE, LANES), F32) for _ in range(sums)]
        + [pltpu.VMEM((parts, PIECE, LANES), F32) for _ in range(sums)],
        compiler_params=pltpu.CompilerParams(collective_id=0, has_side_effects=True, vmem_limit_bytes=56 * 2**20),
    )(send_rows, tile_cols, shifts, start_block, tiles)
    chunk = 2 * tile
    return pl.pallas_call(
        functools.partial(finish_kernel, (steps, width, chunk)),
        out_shape=jax.ShapeDtypeStruct((size, nodes), F32),
        in_specs=[hbm, hbm, hbm, hbm],
        out_specs=hbm,
        scratch_shapes=[
            pltpu.VMEM((width, span), F32),
            pltpu.VMEM((size, size), F32),
            pltpu.VMEM((size, nodes), BF16),
            pltpu.VMEM((done, nodes), F32),
            pltpu.VMEM((width, nodes), F32),
            dma((5 + nodes // chunk,)),
        ],
        compiler_params=pltpu.CompilerParams(vmem_limit_bytes=56 * 2**20),
    )(basis, early, gram, above)


def solution(mesh):
    in_specs = (
        P(None, ("gx", "gy")),
        P(("gx", "gy"), None, None, None),
        P(("gx", "gy"), None),
        P(("gx", "gy"), None),
        P(),
    )
    out_specs = P(None, ("gx", "gy"))
    run = functools.partial(body, mesh.shape["gx"], mesh.shape["gy"])
    return jax.shard_map(run, mesh=mesh, in_specs=in_specs, out_specs=out_specs, check_vma=False)
```
